256 devices in a mesh: sec: 4 (over x_hi, core), dom: 64 (over y, z, x_lo).
Axes of the slice: x: 4 (x_hi: 2, x_lo: 2; x = x_hi * 2 + x_lo), y: 4, z: 8, core: 2. Of those that a mesh axis runs over, the one named last changes fastest.
Arguments:
- actuator_fields: float32 [16, 512, 4096], P(None, 'dom', 'sec'), may hold values from -6 to 6
- sensor_fields: float32 [8, 512, 4096], P(None, 'dom', 'sec'), may hold values from -6 to 6
- region_ids: int32 [512, 4096], P('dom', 'sec'), may hold values from 0 to 15
- stiffness_table: float32 [16], replicated, may hold values from 1 to 4
- density_table: float32 [16], replicated, may hold values from 1 to 2
- supported: int32 [10, 64, 32], P(None, 'dom', 'sec'), may hold values 0 or 1
Outputs:
- final_position: float32 [24, 512, 4096], P(None, 'dom', 'sec')
- cross: float32 [160, 80], P('sec')
The draws below stay inside these ranges and needn't reach their ends.
All inputs are finite; a program needn't handle non-finite values. No bound on the sum of `supported` on one device may be relied on, other than what follows from the above.
Results may differ from the reference program's by a relative error of at most 0.0028.
Values sent between devices are 32-bit elements; how exact they have to be, the bound alone decides.
No kernel may reach another device: no remote copies, remote signals or barrier semaphores. Data moves between devices by JAX's collectives and lax.ppermute only.
A program may use at most 64 MiB of HBM per device.

```python
import math
import jax
import jax.numpy as jnp

CX = 8
TILE_Y = 128
STEPS = 20
ACT = 16
SENS = 8
REGIONS = 16
SNAPS = 10
NX = 512
NY = 4096
N_DOM = 64


def touch_ends(drawn, rng, least, largest):
    spot = [jax.random.randint(jax.random.fold_in(rng, axis), (), 0, length) for axis, length in enumerate(drawn.shape)]
    main_axis = drawn.shape.index(max(drawn.shape))
    neighbour = spot[:main_axis] + [(spot[main_axis] + 1) % drawn.shape[main_axis]] + spot[main_axis + 1:]
    return drawn.at[tuple(spot)].set(least).at[tuple(neighbour)].set(largest)


def block_scale(stream_key, dims, pieces, low, high):
    loudness, own = 1.0, jax.random.fold_in(stream_key, 6)
    for dim, parts in pieces:
        draws = jnp.exp(jax.random.uniform(jax.random.fold_in(own, dim), (parts,), jnp.float32, low / len(pieces), high / len(pieces)))
        loudness = loudness * jnp.repeat(draws, dims[dim] // parts).reshape([-1 if axis == dim else 1 for axis in range(len(dims))])
    return loudness


def scatter_about(stream_key, dims, deviation, limit, cuts=(), dtype=jnp.bfloat16):
    level = block_scale(stream_key, dims, cuts, -0.22, 0.18) if cuts else 1.0
    result = jax.random.normal(stream_key, dims, jnp.float32) * deviation * level
    return jnp.minimum(jnp.maximum(result, -limit), limit).astype(dtype)


def setup_inputs(seed: int = 0) -> dict:
    streams_of = jax.random.split(jax.random.key(seed), 7)
    return {
        "actuator_fields": scatter_about(streams_of[0], (ACT, NX, NY), 1.0, 6.0, ((1, 64), (2, 4)), jnp.float32),
        "sensor_fields": scatter_about(streams_of[1], (SENS, NX, NY), 1.0, 6.0, ((1, 64), (2, 4)), jnp.float32),
        "region_ids": touch_ends(jax.random.randint(streams_of[2], (NX, NY), 0, REGIONS), jax.random.fold_in(streams_of[2], 1), 0, REGIONS - 1).astype(jnp.int32),
        "stiffness_table": jnp.clip(jnp.exp(jax.random.uniform(streams_of[3], (REGIONS,), jnp.float32, math.log(1.0), math.log(4.0))), 1.0, 4.0),
        "density_table": jnp.clip(jnp.exp(jax.random.uniform(streams_of[4], (REGIONS,), jnp.float32, math.log(1.0), math.log(2.0))), 1.0, 2.0),
        "supported": touch_ends((jax.random.randint(streams_of[5], (SNAPS, N_DOM, NY // TILE_Y), 0, 3) < 2).astype(jnp.int32), jax.random.fold_in(streams_of[5], 1), 0, 1),
    }


def divergence(padded, stiff_pad):
    rows = padded.shape[-2] - 2
    cols = padded.shape[-1] - 2
    centre = padded[..., 1:1 + rows, 1:1 + cols]
    stiff_centre = stiff_pad[1:1 + rows, 1:1 + cols]
    total = jnp.zeros_like(centre)
    for first, second in ((0, 1), (2, 1), (1, 0), (1, 2)):
        nearby = padded[..., first:first + rows, second:second + cols]
        stiff_near = stiff_pad[first:first + rows, second:second + cols]
        total = total + 0.5 * (stiff_centre + stiff_near) * (nearby - centre)
    return total

def reference(actuator_fields, sensor_fields, region_ids, stiffness_table, density_table, supported):
    stiffness = stiffness_table[region_ids]
    inv_mass = 1.0 / density_table[region_ids]
    stiff_pad = jnp.pad(stiffness, 1)
    velocity = jnp.concatenate([actuator_fields, sensor_fields], 0) * inv_mass
    position = jnp.zeros_like(velocity)
    frames = []
    for step in range(STEPS):
        padded = jnp.pad(position, ((0, 0), (1, 1), (1, 1)))
        velocity = velocity + 0.35 * inv_mass * divergence(padded, stiff_pad)
        position = position + 0.35 * velocity
        if step % 2 == 1:
            mask_tiles = supported[step // 2]
            cells = jnp.repeat(jnp.repeat(mask_tiles, CX, axis=0), TILE_Y, axis=1).astype(jnp.float32)
            frames.append(jnp.stack([position * cells, velocity * cells], 1).astype(jnp.bfloat16))
    adjoint = jnp.stack([frame[ACT:].reshape(SENS, -1) for frame in frames], 1).reshape(SENS * SNAPS, -1)
    blocks = []
    for frame in frames:
        primal = frame[:ACT].reshape(ACT, -1)
        blocks.append(jnp.dot(primal, adjoint.T, preferred_element_type=jnp.float32))
    joined = jnp.stack(blocks, 1).reshape(ACT * SNAPS, SENS * SNAPS)
    cross = joined * (1.0 / math.sqrt(NX * NY))
    return (position, cross)
```

```python
import math

import jax
import jax.numpy as jnp
from jax import lax
from jax.experimental import pallas as pl
from jax.experimental.pallas import tpu as pltpu
from jax.sharding import PartitionSpec as P

ROWS = 8
COLS = 1024
HALF = 512
LANES = 128
TILES = 5
WIDE = TILES * LANES
HALO = 20
ACT = 16
SENS = 8
RESP = ACT + SENS
SETS = RESP // 8
SNAPS = 10
STEPS = 20
REGIONS = 16
SLABS = ROWS * SETS + 1
NEAR = 3
FAR = NEAR * SETS + 1
OWN = 24
ALL_ROWS = 64
DT = 0.35


def block_column(shape, dim):
    spot = lax.broadcasted_iota(jnp.int32, shape, dim)
    return (spot & (LANES - 1)) * TILES + (spot >> 7)


def split_dot(cells, pick, dims):
    high = cells.astype(jnp.bfloat16)
    low = (cells - high.astype(jnp.float32)).astype(jnp.bfloat16)
    return lax.dot_general(high, pick, dims, preferred_element_type=jnp.float32) + lax.dot_general(
        low, pick, dims, preferred_element_type=jnp.float32
    )


MATMUL = (((1,), (0,)), ((), ()))


def gather_kernel(side_ref, act_ref, sens_ref, ids_ref, left_ref, right_ref, keep_ref, give_ref, rows_ref):
    for row in range(ROWS):
        spot = row * RESP
        rows_ref[spot : spot + ACT, 0:COLS] = act_ref[:, row, :]
        rows_ref[spot + ACT : spot + RESP, 0:COLS] = sens_ref[:, row, :]
        rows_ref[spot : spot + RESP, COLS : COLS + LANES] = left_ref[0:RESP, row, :]
        rows_ref[spot : spot + RESP, COLS + LANES : COLS + 2 * LANES] = right_ref[0:RESP, row, :]
    spot = ROWS * RESP
    rows_ref[spot : spot + ROWS, 0:COLS] = ids_ref[...]
    rows_ref[spot : spot + ROWS, COLS : COLS + LANES] = left_ref[RESP]
    rows_ref[spot : spot + ROWS, COLS + LANES : COLS + 2 * LANES] = right_ref[RESP]
    shape = (WIDE + LANES, WIDE)
    column = block_column(shape, 1)
    source = lax.broadcasted_iota(jnp.int32, shape, 0)
    inner = column < HALF + HALO
    outer = column >= WIDE - HALO
    nowhere = -1
    wanted = jnp.where(inner, column, jnp.where(outer, column + LANES, nowhere))
    pick = jnp.where(source == wanted, 1.0, 0.0).astype(jnp.bfloat16)
    cells = jnp.concatenate([rows_ref[:, 0:WIDE], rows_ref[:, COLS : COLS + LANES]], axis=1)
    first = split_dot(cells, pick, MATMUL).reshape(SLABS, 8, WIDE)
    wanted = jnp.where(inner, column + LANES, jnp.where(outer, column - HALF, nowhere))
    pick = jnp.where(source == wanted, 1.0, 0.0).astype(jnp.bfloat16)
    cells = jnp.concatenate([rows_ref[:, COLS - WIDE : COLS], rows_ref[:, COLS + LANES : COLS + 2 * LANES]], axis=1)
    second = split_dot(cells, pick, MATMUL).reshape(SLABS, 8, WIDE)
    low_side = side_ref[0] == 0
    keep_ref[...] = jnp.where(low_side, first, second)
    give_ref[...] = jnp.where(low_side, second, first)


def after(cells):
    return jnp.concatenate([cells[:, LANES:], pltpu.roll(cells[:, :LANES], LANES - 1, 1)], axis=1)


def before(cells):
    return jnp.concatenate([pltpu.roll(cells[:, WIDE - LANES :], 1, 1), cells[:, : WIDE - LANES]], axis=1)


def wave_kernel(
    side_ref, stiff_ref, dens_ref, sup_ref,
    keep_ref, give_ref, keep_up_ref, give_up_ref, keep_dn_ref, give_dn_ref, far_up_ref, far_dn_ref,
    own_ref, other_ref, cross_ref,
    p_ref, u_ref, s_ref, m_ref, fx_ref, fy_ref, mk_ref, fa_ref, fs_ref, acc_ref,
):
    side = side_ref[0]
    own_base = 8 * side
    other_base = 8 - own_base
    strips = (
        (keep_ref, OWN + own_base), (give_ref, OWN + other_base),
        (keep_up_ref, OWN - 16 + own_base), (give_up_ref, OWN - 16 + other_base),
        (keep_dn_ref, OWN + 16 + own_base), (give_dn_ref, OWN + 16 + other_base),
    )

    def materials(ids, base):
        stiff = jnp.zeros_like(ids)
        dens = jnp.zeros_like(ids)
        for region in range(REGIONS):
            here = ids == region + 1.0
            stiff = jnp.where(here, stiff_ref[region], stiff)
            dens = jnp.where(here, dens_ref[region], dens)
        inside = ids > 0.0
        rows = pl.ds(pl.multiple_of(base, 8), 8)
        s_ref[rows, :] = stiff
        m_ref[rows, :] = jnp.where(inside, (0.5 * DT * DT) / jnp.where(inside, dens, 1.0), 0.0)

    for ref, base in strips:
        materials(ref[SLABS - 1], base)
    materials(far_up_ref[FAR - 1], 0)
    materials(far_dn_ref[FAR - 1], ALL_ROWS - 8)

    def coefficients(row, carry):
        centre = jnp.broadcast_to(s_ref[pl.ds(row, 1), :], (8, WIDE))
        upper = jnp.broadcast_to(s_ref[pl.ds(row - 1, 1), :], (8, WIDE))
        fx_ref[row] = centre + upper
        fy_ref[row] = centre + after(centre)
        mk_ref[row] = jnp.broadcast_to(m_ref[pl.ds(row, 1), :], (8, WIDE))
        return carry

    lax.fori_loop(1, ALL_ROWS, coefficients, 0)

    def place(slab, row, set_index):
        begin = slab * (mk_ref[row] * (DT / (0.5 * DT * DT)))
        u_ref[row * SETS + set_index] = begin
        p_ref[row * SETS + set_index] = begin

    for ref, base in strips:
        def fill(row, carry, ref=ref, base=base):
            for set_index in range(SETS):
                place(ref[row * SETS + set_index], base + row, set_index)
            return carry

        lax.fori_loop(0, ROWS, fill, 0)
    for row in range(NEAR):
        for set_index in range(SETS):
            place(far_up_ref[row * SETS + set_index], 8 - NEAR + row, set_index)
            place(far_dn_ref[row * SETS + set_index], ALL_ROWS - 8 + row, set_index)

    def step(count):
        first = OWN - STEPS + 1 + count
        pairs = (16 + 2 * (STEPS - 1) - 2 * count) // 2
        for set_index in range(SETS):
            centre = p_ref[first * SETS + set_index]
            north = fx_ref[first] * (centre - p_ref[(first - 1) * SETS + set_index])

            def one(row, centre, north, set_index=set_index):
                spot = row * SETS + set_index
                below = p_ref[spot + SETS]
                south = fx_ref[row + 1] * (below - centre)
                east = fy_ref[row] * (after(centre) - centre)
                total = (south - north) + (east - before(east))
                speed = u_ref[spot] + mk_ref[row] * total
                u_ref[spot] = speed
                p_ref[spot] = centre + speed
                return below, south

            def two(pair, carry, one=one):
                row = first + 2 * pair
                carry = one(row, *carry)
                return one(row + 1, *carry)

            lax.fori_loop(0, pairs, two, (centre, north))

    column = block_column((8, WIDE), 1)
    tile = column >> 7

    def snapshot(index):
        act_rows = pl.ds(pl.multiple_of(index * ACT, ACT), ACT)
        sens_rows = pl.ds(pl.multiple_of(index * SENS, SENS), SENS)
        for strip in range(2):
            mask = jnp.zeros((8, WIDE), jnp.float32)
            for part in range(HALF // LANES):
                mask = jnp.where(tile == part, sup_ref[strip, index, (HALF // LANES) * side + part], mask)
            fast = mask * (1.0 / DT)

            def keep_row(row, carry, strip=strip, mask=mask, fast=fast):
                at = row + 8 * strip
                spot = (OWN + at) * SETS
                place_act = jnp.concatenate([p_ref[spot] * mask, p_ref[spot + 1] * mask], axis=0)
                speed_act = jnp.concatenate([u_ref[spot] * fast, u_ref[spot + 1] * fast], axis=0)
                fa_ref[at, act_rows, 0:WIDE] = place_act.astype(jnp.bfloat16)
                fa_ref[at, act_rows, WIDE : 2 * WIDE] = speed_act.astype(jnp.bfloat16)
                fs_ref[at, sens_rows, 0:WIDE] = p_ref[spot + 2] * mask
                fs_ref[at, sens_rows, WIDE : 2 * WIDE] = u_ref[spot + 2] * fast
                return carry

            lax.fori_loop(0, 8, keep_row, 0)

    step(1)
    snapshot(0)

    def advance(index, carry):
        step(2 * index)
        step(2 * index + 1)
        snapshot(index)
        return carry

    lax.fori_loop(1, SNAPS, advance, 0)

    acc_ref[...] = jnp.zeros_like(acc_ref)

    def gram(row, carry):
        acc_ref[...] += lax.dot_general(
            fa_ref[row], fs_ref[row].astype(jnp.bfloat16), (((1,), (1,)), ((), ())), preferred_element_type=jnp.float32
        )
        return carry

    lax.fori_loop(0, 16, gram, 0)
    shape = (ACT * SNAPS, ACT * SNAPS)
    old = lax.broadcasted_iota(jnp.int32, shape, 1)
    new = lax.broadcasted_iota(jnp.int32, shape, 0)
    turn = jnp.where(new == (old & (ACT - 1)) * SNAPS + (old >> 4), 1.0, 0.0)
    shape = (SENS * SNAPS, SENS * SNAPS)
    old = lax.broadcasted_iota(jnp.int32, shape, 0)
    new = lax.broadcasted_iota(jnp.int32, shape, 1)
    turn_back = jnp.where(new == (old & (SENS - 1)) * SNAPS + (old >> 3), 1.0, 0.0)
    exact = dict(precision=lax.Precision.HIGHEST, preferred_element_type=jnp.float32)
    turned = lax.dot_general(turn, acc_ref[...], MATMUL, **exact)
    cross_ref[...] = lax.dot_general(turned, turn_back, MATMUL, **exact)

    shape = (WIDE, HALF)
    pick = jnp.where(
        lax.broadcasted_iota(jnp.int32, shape, 1) == block_column(shape, 0), 1.0, 0.0
    ).astype(jnp.bfloat16)
    for out_ref, base in ((own_ref, OWN + own_base), (other_ref, OWN + other_base)):
        cells = p_ref[pl.ds(base * SETS, ROWS * SETS)].reshape(ROWS * RESP, WIDE)
        cells = split_dot(cells, pick, MATMUL)
        for row in range(ROWS):
            out_ref[:, row, :] = cells[row * RESP : (row + 1) * RESP]


def along_dom(cells, distance):
    count = lax.axis_size("dom")
    return lax.ppermute(cells, "dom", [(i, i + distance) for i in range(count) if 0 <= i + distance < count])


def swap(cells, bit):
    count = lax.axis_size("dom")
    return lax.ppermute(cells, "dom", [(i, i ^ bit) for i in range(count)])


def body(actuator_fields, sensor_fields, region_ids, stiffness_table, density_table, supported):
    side = lax.axis_index("dom") % 2
    side_word = side.astype(jnp.int32).reshape(1)
    ids = region_ids.astype(jnp.float32) + 1.0

    def edge(low):
        high = low + LANES
        return jnp.concatenate(
            [actuator_fields[:, :, low:high], sensor_fields[:, :, low:high], ids[None, :, low:high]], 0
        )

    sections = lax.axis_size("sec")
    left = lax.ppermute(edge(COLS - LANES), "sec", [(i, i + 1) for i in range(sections - 1)])
    right = lax.ppermute(edge(0), "sec", [(i + 1, i) for i in range(sections - 1)])
    sup = supported.reshape(SNAPS, -1).astype(jnp.float32)
    sup_other = swap(sup, 1)
    sup_pair = jnp.where(side == 0, jnp.stack([sup, sup_other]), jnp.stack([sup_other, sup]))

    vmem = pl.BlockSpec(memory_space=pltpu.VMEM)
    smem = pl.BlockSpec(memory_space=pltpu.SMEM)
    block = jax.ShapeDtypeStruct((SLABS, 8, WIDE), jnp.float32)
    keep, give = pl.pallas_call(
        gather_kernel,
        out_shape=(block, block),
        in_specs=[smem] + [vmem] * 5,
        out_specs=(vmem, vmem),
        scratch_shapes=[pltpu.VMEM((ROWS * RESP + ROWS, COLS + 2 * LANES), jnp.float32)],
    )(side_word, actuator_fields, sensor_fields, ids, left, right)

    got = swap(give, 1)
    keep_up, keep_dn = along_dom(keep, 2), along_dom(keep, -2)
    give_up, give_dn = along_dom(got, 2), along_dom(got, -2)
    first_rows = jnp.where(side == 0, keep, got)
    last_rows = jnp.where(side == 0, got, keep)
    near = NEAR * SETS
    far_up = along_dom(last_rows[SLABS - FAR :], 4)
    far_dn = along_dom(jnp.concatenate([first_rows[:near], first_rows[SLABS - 1 :]], 0), -4)

    part = jax.ShapeDtypeStruct((RESP, ROWS, HALF), jnp.float32)
    own, other, local = pl.pallas_call(
        wave_kernel,
        out_shape=(part, part, jax.ShapeDtypeStruct((ACT * SNAPS, SENS * SNAPS), jnp.float32)),
        in_specs=[smem] * 4 + [vmem] * 8,
        out_specs=(vmem, vmem, vmem),
        scratch_shapes=[
            pltpu.VMEM((ALL_ROWS * SETS, 8, WIDE), jnp.float32),
            pltpu.VMEM((ALL_ROWS * SETS, 8, WIDE), jnp.float32),
            pltpu.VMEM((ALL_ROWS, WIDE), jnp.float32),
            pltpu.VMEM((ALL_ROWS, WIDE), jnp.float32),
            pltpu.VMEM((ALL_ROWS, 8, WIDE), jnp.float32),
            pltpu.VMEM((ALL_ROWS, 8, WIDE), jnp.float32),
            pltpu.VMEM((ALL_ROWS, 8, WIDE), jnp.float32),
            pltpu.VMEM((16, ACT * SNAPS, 2 * WIDE), jnp.bfloat16),
            pltpu.VMEM((16, SENS * SNAPS, 2 * WIDE), jnp.float32),
            pltpu.VMEM((ACT * SNAPS, SENS * SNAPS), jnp.float32),
        ],
    )(side_word, stiffness_table, density_table, sup_pair, keep, got, keep_up, give_up, keep_dn, give_dn, far_up, far_dn)

    back = swap(other, 1)
    position = jnp.where(
        side == 0, jnp.concatenate([own, back], 2), jnp.concatenate([back, own], 2)
    )

    share = local.shape[0] // sections
    place = lax.axis_index("sec")
    total = lax.dynamic_slice_in_dim(local, place * share, share, 0)
    for hop in range(1, sections):
        piece = lax.dynamic_slice_in_dim(local, ((place + hop) % sections) * share, share, 0)
        total = total + lax.ppermute(piece, "sec", [(i, (i + hop) % sections) for i in range(sections)])
    bit = 1
    while bit < lax.axis_size("dom"):
        total = total + swap(total, bit)
        bit *= 2
    factor = 1.0 / math.sqrt(ROWS * COLS * sections * lax.axis_size("dom"))
    return (position, total * factor)


def solution(mesh):
    in_specs = (
        P(None, "dom", "sec"),
        P(None, "dom", "sec"),
        P("dom", "sec"),
        P(),
        P(),
        P(None, "dom", "sec"),
    )
    out_specs = (P(None, "dom", "sec"), P("sec", None))
    return jax.shard_map(body, mesh=mesh, in_specs=in_specs, out_specs=out_specs, check_vma=False)
```

```python
import math

import jax
import jax.numpy as jnp
from jax import lax
from jax.experimental import pallas as pl
from jax.experimental.pallas import tpu as pltpu
from jax.sharding import PartitionSpec as P

ROWS = 8
COLS = 1024
HALF = 512
LANES = 128
TILES = 5
WIDE = TILES * LANES
HALO = 20
ACT = 16
SENS = 8
RESP = ACT + SENS
SETS = RESP // 8
SNAPS = 10
STEPS = 20
REGIONS = 16
SLABS = ROWS * SETS + 1
NEAR = 3
FAR = NEAR * SETS + 1
OWN = 24
SHARE = 40
CELLS = 512 * 4096
FLAG_LANE = 112
ALL_ROWS = 64
DT = 0.35


def block_column(shape, dim):
    spot = lax.broadcasted_iota(jnp.int32, shape, dim)
    return (spot & (LANES - 1)) * TILES + (spot >> 7)


MATMUL = (((1,), (0,)), ((), ()))
FAST = dict(preferred_element_type=jnp.float32)
EXACT = dict(precision=lax.Precision.HIGHEST, preferred_element_type=jnp.float32)


def one_hot(hit):
    return jnp.where(hit, 1.0, 0.0).astype(jnp.bfloat16)


def halves(cells):
    high = cells.astype(jnp.bfloat16)
    return high, (cells - high.astype(jnp.float32)).astype(jnp.bfloat16)


def pick_columns(parts, pick):
    return sum(lax.dot_general(part, pick, MATMUL, **FAST) for part in parts)


def turn_rows(parts, turn):
    return [lax.dot_general(turn, part, MATMUL, **FAST).astype(jnp.bfloat16) for part in parts]


def row_major(inverse=False):
    shape = (ROWS * RESP, ROWS * RESP)
    old = lax.broadcasted_iota(jnp.int32, shape, 0 if inverse else 1)
    new = lax.broadcasted_iota(jnp.int32, shape, 1 if inverse else 0)
    return one_hot(new == (old & (ROWS - 1)) * RESP + (old >> 3))


def edge_kernel(*refs):
    for act_ref, sens_ref, ids_ref, out_ref in (refs[0:3] + refs[6:7], refs[3:6] + refs[7:8]):
        out_ref[0:ACT] = act_ref[...]
        out_ref[ACT:RESP] = sens_ref[...]
        out_ref[RESP] = ids_ref[...].astype(jnp.float32) + 1.0


def edges(actuator_fields, sensor_fields, region_ids):
    def blocks(column):
        return [
            pl.BlockSpec((ACT, ROWS, LANES), lambda i, c=column: (0, 0, c)),
            pl.BlockSpec((SENS, ROWS, LANES), lambda i, c=column: (0, 0, c)),
            pl.BlockSpec((ROWS, LANES), lambda i, c=column: (0, c)),
        ]

    out = jax.ShapeDtypeStruct((RESP + 1, ROWS, LANES), jnp.float32)
    whole = pl.BlockSpec((RESP + 1, ROWS, LANES), lambda i: (0, 0, 0))
    fields = (actuator_fields, sensor_fields, region_ids)
    return pl.pallas_call(
        edge_kernel,
        grid=(1,),
        out_shape=(out, out),
        in_specs=blocks(COLS // LANES - 1) + blocks(0),
        out_specs=(whole, whole),
    )(*fields, *fields)


def main_kernel(act_ref, sens_ref, ids_ref, sup_ref, first_ref, second_ref):
    turn = row_major()
    cells = jnp.concatenate(
        [act_ref[...].reshape(ACT * ROWS, COLS), sens_ref[...].reshape(SENS * ROWS, COLS)], axis=0
    )
    parts = turn_rows(halves(cells), turn)
    ids = (ids_ref[...].astype(jnp.float32) + 1.0).astype(jnp.bfloat16)
    shape = (WIDE, WIDE)
    column = block_column(shape, 1)
    source = lax.broadcasted_iota(jnp.int32, shape, 0)
    inner = column < HALF + HALO
    outer = column >= WIDE - HALO
    for out_ref, begin, wanted in (
        (first_ref, 0, jnp.where(inner, column, -1)),
        (second_ref, COLS - WIDE, jnp.where(column < HALF, column + LANES, jnp.where(outer, column - HALF, -1))),
    ):
        pick = one_hot(source == wanted)
        cut = slice(begin, begin + WIDE)
        out_ref[0 : SLABS - 1] = pick_columns([part[:, cut] for part in parts], pick).reshape(SLABS - 1, 8, WIDE)
        out_ref[SLABS - 1] = pick_columns([ids[:, cut]], pick)
        out_ref[SLABS - 1, :, 0:LANES] += sup_ref[...]


def halo_kernel(side_ref, first_ref, second_ref, left_ref, right_ref, keep_ref, give_ref):
    turn = row_major()
    shape = (LANES, WIDE)
    column = block_column(shape, 1)
    source = lax.broadcasted_iota(jnp.int32, shape, 0)
    blocks = []
    for in_ref, edge_ref, hit in (
        (first_ref, left_ref, (column >= WIDE - HALO) & (source == column - HALF)),
        (second_ref, right_ref, (column >= HALF) & (column < HALF + HALO) & (source == column - HALF)),
    ):
        pick = one_hot(hit)
        parts = turn_rows(halves(edge_ref[0:RESP].reshape(RESP * ROWS, LANES)), turn)
        fields = in_ref[0 : SLABS - 1] + pick_columns(parts, pick).reshape(SLABS - 1, 8, WIDE)
        ids = in_ref[SLABS - 1] + pick_columns([edge_ref[RESP].astype(jnp.bfloat16)], pick)
        blocks.append((fields, ids))
    low_side = side_ref[0] == 0
    (fields_0, ids_0), (fields_1, ids_1) = blocks
    keep_ref[0 : SLABS - 1] = jnp.where(low_side, fields_0, fields_1)
    keep_ref[SLABS - 1] = jnp.where(low_side, ids_0, ids_1)
    give_ref[0 : SLABS - 1] = jnp.where(low_side, fields_1, fields_0)
    give_ref[SLABS - 1] = jnp.where(low_side, ids_1, ids_0)


def after(cells):
    return jnp.concatenate([cells[:, LANES:], pltpu.roll(cells[:, :LANES], LANES - 1, 1)], axis=1)


def wave_kernel(
    side_ref, place_ref, stiff_ref, dens_ref,
    keep_ref, give_ref, keep_up_ref, give_up_ref, keep_dn_ref, give_dn_ref, far_up_ref, far_dn_ref,
    own_ref, other_ref, piece_0_ref, piece_1_ref, piece_2_ref, piece_3_ref,
    p_ref, u_ref, s_ref, m_ref, fx_ref, fy_ref, fw_ref, mk_ref, mask_ref, fa_ref, fs_ref, acc_ref,
):
    side = side_ref[0]
    own_base = 8 * side
    other_base = 8 - own_base
    strips = (
        (keep_ref, OWN + own_base), (give_ref, OWN + other_base),
        (keep_up_ref, OWN - 16 + own_base), (give_up_ref, OWN - 16 + other_base),
        (keep_dn_ref, OWN + 16 + own_base), (give_dn_ref, OWN + 16 + other_base),
    )

    def materials(ids, base):
        stiff = jnp.zeros_like(ids)
        dens = jnp.zeros_like(ids)
        for region in range(REGIONS):
            here = ids == region + 1.0
            stiff = jnp.where(here, stiff_ref[region], stiff)
            dens = jnp.where(here, dens_ref[region], dens)
        inside = ids > 0.0
        rows = pl.ds(pl.multiple_of(base, 8), 8)
        s_ref[rows, :] = stiff
        m_ref[rows, :] = jnp.where(inside, (0.5 * DT * DT) / jnp.where(inside, dens, 1.0), 0.0)

    for ref, base in strips:
        materials(ref[SLABS - 1], base)
    shape = (8, WIDE)
    tile = 4 * side + (block_column(shape, 1) >> 7)
    inside = block_column(shape, 1) < HALF
    spread = one_hot(inside & (lax.broadcasted_iota(jnp.int32, shape, 0) == tile))
    for ref, strip in ((keep_ref, side), (give_ref, 1 - side)):
        flags = ref[SLABS - 1, :, 0:LANES].astype(jnp.bfloat16)
        masks = lax.dot_general(flags, spread, (((0,), (0,)), ((), ())), **FAST)
        mask_ref[strip] = masks[FLAG_LANE:LANES]
    materials(far_up_ref[FAR - 1], 0)
    materials(far_dn_ref[FAR - 1], ALL_ROWS - 8)

    def coefficients(row, carry):
        centre = jnp.broadcast_to(s_ref[pl.ds(row, 1), :], (8, WIDE))
        upper = jnp.broadcast_to(s_ref[pl.ds(row - 1, 1), :], (8, WIDE))
        fx_ref[row] = centre + upper
        fy_ref[row] = centre + after(centre)
        fw_ref[row] = centre[:, :LANES] + pltpu.roll(centre[:, WIDE - LANES :], 1, 1)
        mk_ref[row] = jnp.broadcast_to(m_ref[pl.ds(row, 1), :], (8, WIDE))
        return carry

    lax.fori_loop(1, ALL_ROWS, coefficients, 0)

    def place(slab, row, set_index):
        begin = slab * (mk_ref[row] * (DT / (0.5 * DT * DT)))
        u_ref[row * SETS + set_index] = begin
        p_ref[row * SETS + set_index] = begin

    for ref, base in strips:
        def fill(row, carry, ref=ref, base=base):
            for set_index in range(SETS):
                place(ref[row * SETS + set_index], base + row, set_index)
            return carry

        lax.fori_loop(0, ROWS, fill, 0)
    for row in range(NEAR):
        for set_index in range(SETS):
            place(far_up_ref[row * SETS + set_index], 8 - NEAR + row, set_index)
            place(far_dn_ref[row * SETS + set_index], ALL_ROWS - 8 + row, set_index)

    def step(count):
        first = OWN - STEPS + 1 + count
        pairs = (16 + 2 * (STEPS - 1) - 2 * count) // 2

        def start(set_index):
            centre = p_ref[first * SETS + set_index]
            north = fx_ref[first] * (centre - p_ref[(first - 1) * SETS + set_index])
            return centre, north

        def one(row, carry):
            face = fx_ref[row + 1]
            along = fy_ref[row]
            back = fw_ref[row]
            mass = mk_ref[row]
            done = []
            for set_index, (centre, north) in enumerate(carry):
                spot = row * SETS + set_index
                below = p_ref[spot + SETS]
                south = face * (below - centre)
                east = along * (after(centre) - centre)
                first_west = back * (centre[:, :LANES] - pltpu.roll(centre[:, WIDE - LANES :], 1, 1))
                west = jnp.concatenate([first_west, east[:, : WIDE - LANES]], axis=1)
                speed = u_ref[spot] + mass * ((south - north) + (east - west))
                u_ref[spot] = speed
                p_ref[spot] = centre + speed
                done.append((below, south))
            return tuple(done)

        def two(pair, carry):
            row = first + 2 * pair
            return one(row + 1, one(row, carry))

        lax.fori_loop(0, pairs, two, tuple(start(set_index) for set_index in range(SETS)))

    def snapshot(index):
        act_rows = pl.ds(pl.multiple_of(index * ACT, ACT), ACT)
        sens_rows = pl.ds(pl.multiple_of(index * SENS, SENS), SENS)
        for strip in range(2):
            mask = jnp.broadcast_to(mask_ref[strip, pl.ds(index, 1), :], (8, WIDE))
            fast = mask * (1.0 / DT)

            def keep_row(row, carry, strip=strip, mask=mask, fast=fast):
                at = row + 8 * strip
                spot = (OWN + at) * SETS
                place_act = jnp.concatenate([p_ref[spot] * mask, p_ref[spot + 1] * mask], axis=0)
                speed_act = jnp.concatenate([u_ref[spot] * fast, u_ref[spot + 1] * fast], axis=0)
                fa_ref[at, act_rows, 0:WIDE] = place_act.astype(jnp.bfloat16)
                fa_ref[at, act_rows, WIDE : 2 * WIDE] = speed_act.astype(jnp.bfloat16)
                fs_ref[at, sens_rows, 0:WIDE] = p_ref[spot + 2] * mask
                fs_ref[at, sens_rows, WIDE : 2 * WIDE] = u_ref[spot + 2] * fast
                return carry

            lax.fori_loop(0, 8, keep_row, 0)

    step(1)
    snapshot(0)

    def advance(index, carry):
        step(2 * index)
        step(2 * index + 1)
        snapshot(index)
        return carry

    lax.fori_loop(1, SNAPS, advance, 0)

    acc_ref[...] = jnp.zeros_like(acc_ref)

    def gram(row, carry):
        acc_ref[...] += lax.dot_general(
            fa_ref[row], fs_ref[row].astype(jnp.bfloat16), (((1,), (1,)), ((), ())), preferred_element_type=jnp.float32
        )
        return carry

    lax.fori_loop(0, 16, gram, 0)
    shape = (ACT * SNAPS, ACT * SNAPS)
    old = lax.broadcasted_iota(jnp.int32, shape, 1)
    new = lax.broadcasted_iota(jnp.int32, shape, 0)
    turn = jnp.where(new == (old & (ACT - 1)) * SNAPS + (old >> 4), 1.0, 0.0)
    shape = (SENS * SNAPS, SENS * SNAPS)
    old = lax.broadcasted_iota(jnp.int32, shape, 0)
    new = lax.broadcasted_iota(jnp.int32, shape, 1)
    turn_back = jnp.where(new == (old & (SENS - 1)) * SNAPS + (old >> 3), 1.0, 0.0)
    turned = lax.dot_general(turn, acc_ref[...], MATMUL, **EXACT)
    acc_ref[...] = lax.dot_general(turned, turn_back, MATMUL, **EXACT) * (1.0 / math.sqrt(CELLS))
    place = place_ref[0]
    for hop, out_ref in enumerate((piece_0_ref, piece_1_ref, piece_2_ref, piece_3_ref)):
        out_ref[...] = acc_ref[pl.ds(pl.multiple_of(((place + hop) & 3) * SHARE, 8), SHARE), :]

    shape = (WIDE, HALF)
    pick = one_hot(lax.broadcasted_iota(jnp.int32, shape, 1) == block_column(shape, 0))
    turn = row_major(inverse=True)
    for out_ref, base in ((own_ref, OWN + own_base), (other_ref, OWN + other_base)):
        cells = p_ref[pl.ds(base * SETS, ROWS * SETS)].reshape(ROWS * RESP, WIDE)
        out_ref[...] = pick_columns(turn_rows(halves(cells), turn), pick).reshape(RESP, ROWS, HALF)


def advance_block(*operands):
    vmem = pl.BlockSpec(memory_space=pltpu.VMEM)
    smem = pl.BlockSpec(memory_space=pltpu.SMEM)
    part = jax.ShapeDtypeStruct((RESP, ROWS, HALF), jnp.float32)
    return pl.pallas_call(
        wave_kernel,
        out_shape=(part, part) + (jax.ShapeDtypeStruct((SHARE, SENS * SNAPS), jnp.float32),) * 4,
        in_specs=[smem] * 4 + [vmem] * 8,
        out_specs=(vmem,) * 6,
        scratch_shapes=[
            pltpu.VMEM((ALL_ROWS * SETS, 8, WIDE), jnp.float32),
            pltpu.VMEM((ALL_ROWS * SETS, 8, WIDE), jnp.float32),
            pltpu.VMEM((ALL_ROWS, WIDE), jnp.float32),
            pltpu.VMEM((ALL_ROWS, WIDE), jnp.float32),
            pltpu.VMEM((ALL_ROWS, 8, WIDE), jnp.float32),
            pltpu.VMEM((ALL_ROWS, 8, WIDE), jnp.float32),
            pltpu.VMEM((ALL_ROWS, 8, LANES), jnp.float32),
            pltpu.VMEM((ALL_ROWS, 8, WIDE), jnp.float32),
            pltpu.VMEM((2, LANES - FLAG_LANE, WIDE), jnp.float32),
            pltpu.VMEM((16, ACT * SNAPS, 2 * WIDE), jnp.bfloat16),
            pltpu.VMEM((16, SENS * SNAPS, 2 * WIDE), jnp.float32),
            pltpu.VMEM((ACT * SNAPS, SENS * SNAPS), jnp.float32),
        ],
    )(*operands)


def along_dom(cells, distance):
    count = lax.axis_size("dom")
    return lax.ppermute(cells, "dom", [(i, i + distance) for i in range(count) if 0 <= i + distance < count])


def swap(cells, bit):
    count = lax.axis_size("dom")
    return lax.ppermute(cells, "dom", [(i, i ^ bit) for i in range(count)])


def body(actuator_fields, sensor_fields, region_ids, stiffness_table, density_table, supported):
    side = lax.axis_index("dom") % 2
    side_word = side.astype(jnp.int32).reshape(1)
    place_word = lax.axis_index("sec").astype(jnp.int32).reshape(1)
    sections = lax.axis_size("sec")
    right_edge, left_edge = edges(actuator_fields, sensor_fields, region_ids)
    left = lax.ppermute(right_edge, "sec", [(i, i + 1) for i in range(sections - 1)])
    right = lax.ppermute(left_edge, "sec", [(i + 1, i) for i in range(sections - 1)])
    flags = supported.reshape(SNAPS, -1).T.astype(jnp.float32)
    flags = jnp.pad(flags, ((0, 0), (FLAG_LANE, LANES - FLAG_LANE - SNAPS)))

    vmem = pl.BlockSpec(memory_space=pltpu.VMEM)
    smem = pl.BlockSpec(memory_space=pltpu.SMEM)
    block = jax.ShapeDtypeStruct((SLABS, 8, WIDE), jnp.float32)
    first, second = pl.pallas_call(
        main_kernel, out_shape=(block, block), in_specs=[vmem] * 4, out_specs=(vmem, vmem)
    )(actuator_fields, sensor_fields, region_ids, flags)
    keep, give = pl.pallas_call(
        halo_kernel, out_shape=(block, block), in_specs=[smem] + [vmem] * 4, out_specs=(vmem, vmem)
    )(side_word, first, second, left, right)

    got = swap(give, 1)
    keep_up, keep_dn = along_dom(keep, 2), along_dom(keep, -2)
    give_up, give_dn = along_dom(got, 2), along_dom(got, -2)
    near = NEAR * SETS
    cut = SLABS - FAR
    last_rows = jnp.where(side == 0, got[cut:], keep[cut:])
    first_rows = jnp.where(side == 0, keep[:near], got[:near])
    first_ids = jnp.where(side == 0, keep[SLABS - 1 :], got[SLABS - 1 :])
    far_up = along_dom(last_rows, 4)
    far_dn = along_dom(jnp.concatenate([first_rows, first_ids], 0), -4)

    own, other, *pieces = advance_block(
        side_word, place_word, stiffness_table, density_table,
        keep, got, keep_up, give_up, keep_dn, give_dn, far_up, far_dn,
    )
    total = pieces[0]
    for hop in range(1, sections):
        total = total + lax.ppermute(pieces[hop], "sec", [(i, (i + hop) % sections) for i in range(sections)])
    other, total = lax.optimization_barrier((other, total))
    back = swap(other, 1)
    position = jnp.where(
        side == 0, jnp.concatenate([own, back], 2), jnp.concatenate([back, own], 2)
    )
    for bits in (2, 4, 12, 16, 48, 1):
        total = total + swap(total, bits)
    return (position, total)


def solution(mesh):
    in_specs = (
        P(None, "dom", "sec"),
        P(None, "dom", "sec"),
        P("dom", "sec"),
        P(),
        P(),
        P(None, "dom", "sec"),
    )
    out_specs = (P(None, "dom", "sec"), P("sec", None))
    return jax.shard_map(body, mesh=mesh, in_specs=in_specs, out_specs=out_specs, check_vma=False)
```

```python
import math

import jax
import jax.numpy as jnp
from jax import lax
from jax.experimental import pallas as pl
from jax.experimental.pallas import tpu as pltpu
from jax.sharding import PartitionSpec as P


ROWS = 8
COLS = 1024
HALF = 512
LANES = 128
TILES = 5
WIDE = TILES * LANES
HALO = 20
ACT = 16
SENS = 8
RESP = ACT + SENS
SETS = RESP // 8
SNAPS = 10
STEPS = 20
REGIONS = 16
SLABS = ROWS * SETS + 1
NEAR = 3
FAR = NEAR * SETS + 1
OWN = 24
SHARE = 40
CELLS = 512 * 4096
FLAG_LANE = 112
UNROLL = 4
ALL_ROWS = 64
DT = 0.35


def block_column(shape, dim):
    spot = lax.broadcasted_iota(jnp.int32, shape, dim)
    return (spot & (LANES - 1)) * TILES + (spot >> 7)


MATMUL = (((1,), (0,)), ((), ()))
FAST = dict(preferred_element_type=jnp.float32)
EXACT = dict(precision=lax.Precision.HIGHEST, preferred_element_type=jnp.float32)


def one_hot(hit):
    return jnp.where(hit, 1.0, 0.0).astype(jnp.bfloat16)


def halves(cells):
    high = cells.astype(jnp.bfloat16)
    return high, (cells - high.astype(jnp.float32)).astype(jnp.bfloat16)


def pick_columns(parts, pick):
    return sum(lax.dot_general(part, pick, MATMUL, **FAST) for part in parts)


def turn_rows(parts, turn):
    return [lax.dot_general(turn, part, MATMUL, **FAST).astype(jnp.bfloat16) for part in parts]


def row_major(inverse=False):
    shape = (ROWS * RESP, ROWS * RESP)
    old = lax.broadcasted_iota(jnp.int32, shape, 0 if inverse else 1)
    new = lax.broadcasted_iota(jnp.int32, shape, 1 if inverse else 0)
    return one_hot(new == (old & (ROWS - 1)) * RESP + (old >> 3))


def edge_kernel(*refs):
    for act_ref, sens_ref, ids_ref, out_ref in (refs[0:3] + refs[6:7], refs[3:6] + refs[7:8]):
        out_ref[0:ACT] = act_ref[...]
        out_ref[ACT:RESP] = sens_ref[...]
        out_ref[RESP] = ids_ref[...].astype(jnp.float32) + 1.0


def edges(actuator_fields, sensor_fields, region_ids):
    def blocks(column):
        return [
            pl.BlockSpec((ACT, ROWS, LANES), lambda i, c=column: (0, 0, c)),
            pl.BlockSpec((SENS, ROWS, LANES), lambda i, c=column: (0, 0, c)),
            pl.BlockSpec((ROWS, LANES), lambda i, c=column: (0, c)),
        ]

    out = jax.ShapeDtypeStruct((RESP + 1, ROWS, LANES), jnp.float32)
    whole = pl.BlockSpec((RESP + 1, ROWS, LANES), lambda i: (0, 0, 0))
    fields = (actuator_fields, sensor_fields, region_ids)
    return pl.pallas_call(
        edge_kernel,
        grid=(1,),
        out_shape=(out, out),
        in_specs=blocks(COLS // LANES - 1) + blocks(0),
        out_specs=(whole, whole),
    )(*fields, *fields)


def main_kernel(act_ref, sens_ref, ids_ref, sup_ref, first_ref, second_ref):
    turn = row_major()
    cells = jnp.concatenate(
        [act_ref[...].reshape(ACT * ROWS, COLS), sens_ref[...].reshape(SENS * ROWS, COLS)], axis=0
    )
    parts = turn_rows(halves(cells), turn)
    ids = (ids_ref[...].astype(jnp.float32) + 1.0).astype(jnp.bfloat16)
    shape = (WIDE, WIDE)
    column = block_column(shape, 1)
    source = lax.broadcasted_iota(jnp.int32, shape, 0)
    inner = column < HALF + HALO
    outer = column >= WIDE - HALO
    for out_ref, begin, wanted in (
        (first_ref, 0, jnp.where(inner, column, -1)),
        (second_ref, COLS - WIDE, jnp.where(column < HALF, column + LANES, jnp.where(outer, column - HALF, -1))),
    ):
        pick = one_hot(source == wanted)
        cut = slice(begin, begin + WIDE)
        out_ref[0 : SLABS - 1] = pick_columns([part[:, cut] for part in parts], pick).reshape(SLABS - 1, 8, WIDE)
        out_ref[SLABS - 1] = pick_columns([ids[:, cut]], pick)
        out_ref[SLABS - 1, :, FLAG_LANE : FLAG_LANE + SNAPS] = sup_ref[...].astype(jnp.float32)


def halo_kernel(side_ref, first_ref, second_ref, left_ref, right_ref, keep_ref, give_ref, far_keep_ref, far_give_ref):
    turn = row_major()
    shape = (LANES, WIDE)
    column = block_column(shape, 1)
    source = lax.broadcasted_iota(jnp.int32, shape, 0)
    blocks = []
    for in_ref, edge_ref, hit in (
        (first_ref, left_ref, (column >= WIDE - HALO) & (source == column - HALF)),
        (second_ref, right_ref, (column >= HALF) & (column < HALF + HALO) & (source == column - HALF)),
    ):
        pick = one_hot(hit)
        parts = turn_rows(halves(edge_ref[0:RESP].reshape(RESP * ROWS, LANES)), turn)
        fields = in_ref[0 : SLABS - 1] + pick_columns(parts, pick).reshape(SLABS - 1, 8, WIDE)
        ids = in_ref[SLABS - 1] + pick_columns([edge_ref[RESP].astype(jnp.bfloat16)], pick)
        blocks.append((fields, ids))
    low_side = side_ref[0] == 0
    (fields_0, ids_0), (fields_1, ids_1) = blocks
    near = NEAR * SETS
    for out_ref, far_ref, fields, ids in (
        (keep_ref, far_keep_ref, jnp.where(low_side, fields_0, fields_1), jnp.where(low_side, ids_0, ids_1)),
        (give_ref, far_give_ref, jnp.where(low_side, fields_1, fields_0), jnp.where(low_side, ids_1, ids_0)),
    ):
        out_ref[0 : SLABS - 1] = fields
        out_ref[SLABS - 1] = ids
        far_ref[0:near] = jnp.where(low_side, fields[:near], fields[SLABS - 1 - near :])
        far_ref[near] = ids


def after(cells):
    return jnp.concatenate([cells[:, LANES:], pltpu.roll(cells[:, :LANES], LANES - 1, 1)], axis=1)


def wave_kernel(
    side_ref, place_ref, stiff_ref, dens_ref,
    keep_ref, give_ref, keep_up_ref, give_up_ref, keep_dn_ref, give_dn_ref, far_keep_ref, far_give_ref,
    own_ref, other_ref, piece_0_ref, piece_1_ref, piece_2_ref, piece_3_ref,
    p_ref, u_ref, s_ref, m_ref, fx_ref, fy_ref, fw_ref, mk_ref, mask_ref, fa_ref, fs_ref, acc_ref,
):
    side = side_ref[0]
    own_base = 8 * side
    other_base = 8 - own_base
    strips = (
        (keep_ref, OWN + own_base), (give_ref, OWN + other_base),
        (keep_up_ref, OWN - 16 + own_base), (give_up_ref, OWN - 16 + other_base),
        (keep_dn_ref, OWN + 16 + own_base), (give_dn_ref, OWN + 16 + other_base),
    )

    def materials(ids, base):
        stiff = jnp.zeros_like(ids)
        dens = jnp.zeros_like(ids)
        for region in range(REGIONS):
            here = ids == region + 1.0
            stiff = jnp.where(here, stiff_ref[region], stiff)
            dens = jnp.where(here, dens_ref[region], dens)
        inside = ids > 0.0
        rows = pl.ds(pl.multiple_of(base, 8), 8)
        s_ref[rows, :] = stiff
        m_ref[rows, :] = jnp.where(inside, (0.5 * DT * DT) / jnp.where(inside, dens, 1.0), 0.0)

    for ref, base in strips:
        materials(ref[SLABS - 1], base)
    shape = (8, WIDE)
    tile = 4 * side + (block_column(shape, 1) >> 7)
    inside = block_column(shape, 1) < HALF
    spread = one_hot(inside & (lax.broadcasted_iota(jnp.int32, shape, 0) == tile))
    for ref, strip in ((keep_ref, side), (give_ref, 1 - side)):
        flags = ref[SLABS - 1, :, 0:LANES].astype(jnp.bfloat16)
        masks = lax.dot_general(flags, spread, (((0,), (0,)), ((), ())), **FAST)
        mask_ref[strip] = masks[FLAG_LANE:LANES]
    last_strip = ALL_ROWS - 8
    far = ((far_keep_ref, side), (far_give_ref, 1 - side))
    for ref, above in far:
        materials(ref[FAR - 1], last_strip * (1 - above))

    def coefficients(turn, carry):
        for extra in range(9):
            row = 1 + turn * 9 + extra
            centre = jnp.broadcast_to(s_ref[pl.ds(row, 1), :], (8, WIDE))
            upper = jnp.broadcast_to(s_ref[pl.ds(row - 1, 1), :], (8, WIDE))
            fx_ref[row] = centre + upper
            fy_ref[row] = centre + after(centre)
            fw_ref[row] = centre[:, :LANES] + pltpu.roll(centre[:, WIDE - LANES :], 1, 1)
            mk_ref[row] = jnp.broadcast_to(m_ref[pl.ds(row, 1), :], (8, WIDE))
        return carry

    lax.fori_loop(0, (ALL_ROWS - 1) // 9, coefficients, 0)

    def place(slab, row, set_index):
        begin = slab * (mk_ref[row] * (DT / (0.5 * DT * DT)))
        u_ref[row * SETS + set_index] = begin
        p_ref[row * SETS + set_index] = begin

    for ref, base in strips:
        def fill(row, carry, ref=ref, base=base):
            for set_index in range(SETS):
                place(ref[row * SETS + set_index], base + row, set_index)
            return carry

        lax.fori_loop(0, ROWS, fill, 0)
    for ref, above in far:
        base = above * (8 - NEAR) + last_strip * (1 - above)
        for row in range(NEAR):
            for set_index in range(SETS):
                place(ref[row * SETS + set_index], base + row, set_index)

    def step(count):
        first = OWN - STEPS + 1 + count
        rows = 16 + 2 * (STEPS - 1) - 2 * count

        def start(set_index):
            centre = p_ref[first * SETS + set_index]
            north = fx_ref[first] * (centre - p_ref[(first - 1) * SETS + set_index])
            return centre, north

        def one(row, carry):
            face = fx_ref[row + 1]
            along = fy_ref[row]
            back = fw_ref[row]
            mass = mk_ref[row]
            done = []
            for set_index, (centre, north) in enumerate(carry):
                spot = row * SETS + set_index
                below = p_ref[spot + SETS]
                south = face * (below - centre)
                east = along * (after(centre) - centre)
                first_west = back * (centre[:, :LANES] - pltpu.roll(centre[:, WIDE - LANES :], 1, 1))
                west = jnp.concatenate([first_west, east[:, : WIDE - LANES]], axis=1)
                speed = u_ref[spot] + mass * ((south - north) + (east - west))
                u_ref[spot] = speed
                p_ref[spot] = centre + speed
                done.append((below, south))
            return tuple(done)

        def several(turn, carry):
            row = first + UNROLL * turn
            for extra in range(UNROLL):
                carry = one(row + extra, carry)
            return carry

        begin = tuple(start(set_index) for set_index in range(SETS))
        lax.fori_loop(0, (rows + UNROLL - 1) // UNROLL, several, begin)

    def snapshot(index):
        act_rows = pl.ds(pl.multiple_of(index * ACT, ACT), ACT)
        sens_rows = pl.ds(pl.multiple_of(index * SENS, SENS), SENS)
        for strip in range(2):
            mask = jnp.broadcast_to(mask_ref[strip, pl.ds(index, 1), :], (8, WIDE))
            fast = mask * (1.0 / DT)

            def keep_rows(turn, carry, strip=strip, mask=mask, fast=fast):
                for extra in range(4):
                    at = turn * 4 + extra + 8 * strip
                    spot = (OWN + at) * SETS
                    place_act = jnp.concatenate([p_ref[spot] * mask, p_ref[spot + 1] * mask], axis=0)
                    speed_act = jnp.concatenate([u_ref[spot] * fast, u_ref[spot + 1] * fast], axis=0)
                    fa_ref[at, act_rows, 0:WIDE] = place_act.astype(jnp.bfloat16)
                    fa_ref[at, act_rows, WIDE : 2 * WIDE] = speed_act.astype(jnp.bfloat16)
                    fs_ref[at, sens_rows, 0:WIDE] = p_ref[spot + 2] * mask
                    fs_ref[at, sens_rows, WIDE : 2 * WIDE] = u_ref[spot + 2] * fast
                return carry

            lax.fori_loop(0, 2, keep_rows, 0)

    step(1)
    snapshot(0)

    def advance(index, carry):
        step(2 * index)
        step(2 * index + 1)
        snapshot(index)
        return carry

    lax.fori_loop(1, SNAPS, advance, 0)

    def gram(turn, total):
        for extra in range(4):
            row = 4 * turn + extra
            total = total + lax.dot_general(
                fa_ref[row], fs_ref[row].astype(jnp.bfloat16), (((1,), (1,)), ((), ())), **FAST
            )
        return total

    acc_ref[...] = lax.fori_loop(0, 4, gram, jnp.zeros((ACT * SNAPS, SENS * SNAPS), jnp.float32))
    shape = (ACT * SNAPS, ACT * SNAPS)
    old = lax.broadcasted_iota(jnp.int32, shape, 1)
    new = lax.broadcasted_iota(jnp.int32, shape, 0)
    turn = jnp.where(new == (old & (ACT - 1)) * SNAPS + (old >> 4), 1.0, 0.0)
    shape = (SENS * SNAPS, SENS * SNAPS)
    old = lax.broadcasted_iota(jnp.int32, shape, 0)
    new = lax.broadcasted_iota(jnp.int32, shape, 1)
    turn_back = jnp.where(new == (old & (SENS - 1)) * SNAPS + (old >> 3), 1.0, 0.0)
    turned = lax.dot_general(turn, acc_ref[...], MATMUL, **EXACT)
    acc_ref[...] = lax.dot_general(turned, turn_back, MATMUL, **EXACT) * (1.0 / math.sqrt(CELLS))
    place = place_ref[0]
    for hop, out_ref in enumerate((piece_0_ref, piece_1_ref, piece_2_ref, piece_3_ref)):
        out_ref[...] = acc_ref[pl.ds(pl.multiple_of(((place + hop) & 3) * SHARE, 8), SHARE), :]

    shape = (WIDE, HALF)
    pick = one_hot(lax.broadcasted_iota(jnp.int32, shape, 1) == block_column(shape, 0))
    turn = row_major(inverse=True)
    for out_ref, base in ((own_ref, OWN + own_base), (other_ref, OWN + other_base)):
        cells = p_ref[pl.ds(base * SETS, ROWS * SETS)].reshape(ROWS * RESP, WIDE)
        out_ref[...] = pick_columns(turn_rows(halves(cells), turn), pick).reshape(RESP, ROWS, HALF)


def advance_block(*operands):
    vmem = pl.BlockSpec(memory_space=pltpu.VMEM)
    smem = pl.BlockSpec(memory_space=pltpu.SMEM)
    part = jax.ShapeDtypeStruct((RESP, ROWS, HALF), jnp.float32)
    return pl.pallas_call(
        wave_kernel,
        out_shape=(part, part) + (jax.ShapeDtypeStruct((SHARE, SENS * SNAPS), jnp.float32),) * 4,
        in_specs=[smem] * 4 + [vmem] * 8,
        out_specs=(vmem,) * 6,
        scratch_shapes=[
            pltpu.VMEM((ALL_ROWS * SETS, 8, WIDE), jnp.float32),
            pltpu.VMEM((ALL_ROWS * SETS, 8, WIDE), jnp.float32),
            pltpu.VMEM((ALL_ROWS, WIDE), jnp.float32),
            pltpu.VMEM((ALL_ROWS, WIDE), jnp.float32),
            pltpu.VMEM((ALL_ROWS, 8, WIDE), jnp.float32),
            pltpu.VMEM((ALL_ROWS, 8, WIDE), jnp.float32),
            pltpu.VMEM((ALL_ROWS, 8, LANES), jnp.float32),
            pltpu.VMEM((ALL_ROWS, 8, WIDE), jnp.float32),
            pltpu.VMEM((2, LANES - FLAG_LANE, WIDE), jnp.float32),
            pltpu.VMEM((16, ACT * SNAPS, 2 * WIDE), jnp.bfloat16),
            pltpu.VMEM((16, SENS * SNAPS, 2 * WIDE), jnp.float32),
            pltpu.VMEM((ACT * SNAPS, SENS * SNAPS), jnp.float32),
        ],
        compiler_params=grant(40),
    )(*operands)


def along_dom(cells, distance):
    count = lax.axis_size("dom")
    return lax.ppermute(cells, "dom", [(i, i + distance) for i in range(count) if 0 <= i + distance < count])


def outward(cells, distance):
    count = lax.axis_size("dom")
    pairs = [(i, i + distance if i % 2 else i - distance) for i in range(count)]
    return lax.ppermute(cells, "dom", [(i, j) for i, j in pairs if 0 <= j < count])


def grant(mebibytes):
    return pltpu.CompilerParams(vmem_limit_bytes=mebibytes << 20)


def swap(cells, bit):
    count = lax.axis_size("dom")
    return lax.ppermute(cells, "dom", [(i, i ^ bit) for i in range(count)])


def body(actuator_fields, sensor_fields, region_ids, stiffness_table, density_table, supported):
    side = lax.axis_index("dom") % 2
    side_word = side.astype(jnp.int32).reshape(1)
    place_word = lax.axis_index("sec").astype(jnp.int32).reshape(1)
    sections = lax.axis_size("sec")
    right_edge, left_edge = edges(actuator_fields, sensor_fields, region_ids)
    left = lax.ppermute(right_edge, "sec", [(i, i + 1) for i in range(sections - 1)])
    right = lax.ppermute(left_edge, "sec", [(i + 1, i) for i in range(sections - 1)])
    flags = jnp.transpose(supported, (1, 2, 0)).reshape(-1, SNAPS)

    vmem = pl.BlockSpec(memory_space=pltpu.VMEM)
    smem = pl.BlockSpec(memory_space=pltpu.SMEM)
    block = jax.ShapeDtypeStruct((SLABS, 8, WIDE), jnp.float32)
    first, second = pl.pallas_call(
        main_kernel, out_shape=(block, block), in_specs=[vmem] * 4, out_specs=(vmem, vmem), compiler_params=grant(16)
    )(actuator_fields, sensor_fields, region_ids, flags)
    far = jax.ShapeDtypeStruct((FAR, 8, WIDE), jnp.float32)
    keep, give, far_keep, far_give = pl.pallas_call(
        halo_kernel,
        out_shape=(block, block, far, far),
        in_specs=[smem] + [vmem] * 4,
        out_specs=(vmem,) * 4,
        compiler_params=grant(16),
    )(side_word, first, second, left, right)

    got = swap(give, 1)
    keep_up, keep_dn = along_dom(keep, 2), along_dom(keep, -2)
    far_keep = outward(far_keep, 4)
    far_give = outward(far_give, 3)
    give_up = along_dom(got, 2)
    give_dn = along_dom(got, -2)

    own, other, *pieces = advance_block(
        side_word, place_word, stiffness_table, density_table,
        keep, got, keep_up, give_up, keep_dn, give_dn, far_keep, far_give,
    )
    total = pieces[0]
    for hop in range(1, sections):
        total = total + lax.ppermute(pieces[hop], "sec", [(i, (i + hop) % sections) for i in range(sections)])
    other, total = lax.optimization_barrier((other, total))
    back = swap(other, 1)
    position = jnp.where(
        side == 0, jnp.concatenate([own, back], 2), jnp.concatenate([back, own], 2)
    )
    for bits in (4, 12, 16, 48):
        total = total + swap(total, bits)
    position, total = lax.optimization_barrier((position, total))
    total = total + sum(swap(total, bits) for bits in (1, 2, 3))
    return (position, total)


def solution(mesh):
    in_specs = (
        P(None, "dom", "sec"),
        P(None, "dom", "sec"),
        P("dom", "sec"),
        P(),
        P(),
        P(None, "dom", "sec"),
    )
    out_specs = (P(None, "dom", "sec"), P("sec", None))
    return jax.shard_map(body, mesh=mesh, in_specs=in_specs, out_specs=out_specs, check_vma=False)
```

```python
import math

import jax
import jax.numpy as jnp
from jax import lax
from jax.experimental import pallas as pl
from jax.experimental.pallas import tpu as pltpu
from jax.sharding import PartitionSpec as P


ROWS = 8
COLS = 1024
HALF = 512
LANES = 128
TILES = 5
WIDE = TILES * LANES
HALO = 20
ACT = 16
SENS = 8
RESP = ACT + SENS
SETS = RESP // 8
SNAPS = 10
STEPS = 20
REGIONS = 16
SLABS = ROWS * SETS + 1
NEAR = 3
FAR = NEAR * SETS + 1
OWN = 24
SHARE = 40
CELLS = 512 * 4096
FLAG_LANE = 112
ACT_SETS = ACT // 8
CENTRE_ROWS = 2 * ROWS
SENS_SLABS = ROWS + 1
ACT_SLABS = ROWS * ACT_SETS
ALL_ROWS = 64
DT = 0.35


def block_column(shape, dim):
    spot = lax.broadcasted_iota(jnp.int32, shape, dim)
    return (spot & (LANES - 1)) * TILES + (spot >> 7)


MATMUL = (((1,), (0,)), ((), ()))
FAST = dict(preferred_element_type=jnp.float32)
EXACT = dict(precision=lax.Precision.HIGHEST, preferred_element_type=jnp.float32)


def one_hot(hit):
    return jnp.where(hit, 1.0, 0.0).astype(jnp.bfloat16)


def halves(cells):
    high = cells.astype(jnp.bfloat16)
    return high, (cells - high.astype(jnp.float32)).astype(jnp.bfloat16)


def pick_columns(parts, pick):
    return sum(lax.dot_general(part, pick, MATMUL, **FAST) for part in parts)


def turn_rows(parts, turn):
    return [lax.dot_general(turn, part, MATMUL, **FAST).astype(jnp.bfloat16) for part in parts]


def row_major(count=RESP, inverse=False):
    shape = (ROWS * count, ROWS * count)
    old = lax.broadcasted_iota(jnp.int32, shape, 0 if inverse else 1)
    new = lax.broadcasted_iota(jnp.int32, shape, 1 if inverse else 0)
    return one_hot(new == (old & (ROWS - 1)) * count + (old >> 3))


def edge_kernel(*refs):
    for act_ref, sens_ref, ids_ref, out_ref in (refs[0:3] + refs[6:7], refs[3:6] + refs[7:8]):
        out_ref[0:ACT] = act_ref[...]
        out_ref[ACT:RESP] = sens_ref[...]
        out_ref[RESP] = ids_ref[...].astype(jnp.float32) + 1.0


def edges(actuator_fields, sensor_fields, region_ids):
    def blocks(column):
        return [
            pl.BlockSpec((ACT, ROWS, LANES), lambda i, c=column: (0, 0, c)),
            pl.BlockSpec((SENS, ROWS, LANES), lambda i, c=column: (0, 0, c)),
            pl.BlockSpec((ROWS, LANES), lambda i, c=column: (0, c)),
        ]

    out = jax.ShapeDtypeStruct((RESP + 1, ROWS, LANES), jnp.float32)
    whole = pl.BlockSpec((RESP + 1, ROWS, LANES), lambda i: (0, 0, 0))
    fields = (actuator_fields, sensor_fields, region_ids)
    return pl.pallas_call(
        edge_kernel,
        grid=(1,),
        out_shape=(out, out),
        in_specs=blocks(COLS // LANES - 1) + blocks(0),
        out_specs=(whole, whole),
    )(*fields, *fields)


def main_kernel(act_ref, sens_ref, ids_ref, sup_ref, first_ref, second_ref):
    turn = row_major()
    cells = jnp.concatenate(
        [act_ref[...].reshape(ACT * ROWS, COLS), sens_ref[...].reshape(SENS * ROWS, COLS)], axis=0
    )
    parts = turn_rows(halves(cells), turn)
    ids = (ids_ref[...].astype(jnp.float32) + 1.0).astype(jnp.bfloat16)
    shape = (WIDE, WIDE)
    column = block_column(shape, 1)
    source = lax.broadcasted_iota(jnp.int32, shape, 0)
    inner = column < HALF + HALO
    outer = column >= WIDE - HALO
    for out_ref, begin, wanted in (
        (first_ref, 0, jnp.where(inner, column, -1)),
        (second_ref, COLS - WIDE, jnp.where(column < HALF, column + LANES, jnp.where(outer, column - HALF, -1))),
    ):
        pick = one_hot(source == wanted)
        cut = slice(begin, begin + WIDE)
        out_ref[0 : SLABS - 1] = pick_columns([part[:, cut] for part in parts], pick).reshape(SLABS - 1, 8, WIDE)
        out_ref[SLABS - 1] = pick_columns([ids[:, cut]], pick)
        out_ref[SLABS - 1, :, FLAG_LANE : FLAG_LANE + SNAPS] = sup_ref[...].astype(jnp.float32)


def halo_kernel(side_ref, first_ref, second_ref, left_ref, right_ref, *out_refs):
    turn = row_major()
    shape = (LANES, WIDE)
    column = block_column(shape, 1)
    source = lax.broadcasted_iota(jnp.int32, shape, 0)
    blocks = []
    for in_ref, edge_ref, hit in (
        (first_ref, left_ref, (column >= WIDE - HALO) & (source == column - HALF)),
        (second_ref, right_ref, (column >= HALF) & (column < HALF + HALO) & (source == column - HALF)),
    ):
        pick = one_hot(hit)
        parts = turn_rows(halves(edge_ref[0:RESP].reshape(RESP * ROWS, LANES)), turn)
        fields = in_ref[0 : SLABS - 1] + pick_columns(parts, pick).reshape(SLABS - 1, 8, WIDE)
        ids = in_ref[SLABS - 1] + pick_columns([edge_ref[RESP].astype(jnp.bfloat16)], pick)
        blocks.append((fields, ids))
    low_side = side_ref[0] == 0
    (fields_0, ids_0), (fields_1, ids_1) = blocks
    near = NEAR * SETS
    keep_s_ref, keep_a_ref, give_ref, far_keep_ref, far_give_ref = out_refs
    for sens_ref, act_ref, far_ref, fields, ids in (
        (keep_s_ref, keep_a_ref, far_keep_ref, jnp.where(low_side, fields_0, fields_1), jnp.where(low_side, ids_0, ids_1)),
        (
            give_ref.at[0:SENS_SLABS], give_ref.at[SENS_SLABS:], far_give_ref,
            jnp.where(low_side, fields_1, fields_0), jnp.where(low_side, ids_1, ids_0),
        ),
    ):
        grid = fields.reshape(ROWS, SETS, 8, WIDE)
        act_ref[...] = grid[:, :ACT_SETS].reshape(ACT_SLABS, 8, WIDE)
        sens_ref[0:ROWS] = grid[:, ACT_SETS]
        sens_ref[ROWS] = ids
        far_ref[0:near] = jnp.where(low_side, fields[:near], fields[SLABS - 1 - near :])
        far_ref[near] = ids


def after(cells):
    return jnp.concatenate([cells[:, LANES:], pltpu.roll(cells[:, :LANES], LANES - 1, 1)], axis=1)


def strip_bases(side):
    return [OWN + shift + spot for shift in (0, -16, 16) for spot in (8 * side, 8 - 8 * side)]


def fill(side, strips, far, sets, offset, p_ref, u_ref, mk_ref):
    def place(slab, row, spot):
        begin = slab * (mk_ref[row] * (DT / (0.5 * DT * DT)))
        u_ref[spot] = begin
        p_ref[spot] = begin

    for ref, base in zip(strips, strip_bases(side)):
        def fill_row(row, carry, ref=ref, base=base):
            for index in range(sets):
                place(ref[row * sets + index], base + row, (base + row) * sets + index)
            return carry

        lax.fori_loop(0, ROWS, fill_row, 0)
    for ref, above in zip(far, (side, 1 - side)):
        base = above * (8 - NEAR) + (ALL_ROWS - 8) * (1 - above)
        for row in range(NEAR):
            for index in range(sets):
                place(ref[row * SETS + offset + index], base + row, (base + row) * sets + index)


def step(count, sets, unroll, p_ref, u_ref, fx_ref, fy_ref, fw_ref, mk_ref):
    first = OWN - STEPS + 1 + count
    rows = CENTRE_ROWS + 2 * (STEPS - 1) - 2 * count

    def start(index):
        centre = p_ref[first * sets + index]
        north = fx_ref[first] * (centre - p_ref[(first - 1) * sets + index])
        return centre, north

    def one(row, carry):
        face = fx_ref[row + 1]
        along = fy_ref[row]
        back = fw_ref[row]
        mass = mk_ref[row]
        done = []
        for index, (centre, north) in enumerate(carry):
            spot = row * sets + index
            below = p_ref[spot + sets]
            south = face * (below - centre)
            east = along * (after(centre) - centre)
            first_west = back * (centre[:, :LANES] - pltpu.roll(centre[:, WIDE - LANES :], 1, 1))
            west = jnp.concatenate([first_west, east[:, : WIDE - LANES]], axis=1)
            speed = u_ref[spot] + mass * ((south - north) + (east - west))
            u_ref[spot] = speed
            p_ref[spot] = centre + speed
            done.append((below, south))
        return tuple(done)

    def several(turn, carry):
        row = first + unroll * turn
        for extra in range(unroll):
            carry = one(row + extra, carry)
        return carry

    lax.fori_loop(0, (rows + unroll - 1) // unroll, several, tuple(start(index) for index in range(sets)))


def march(sets, unroll, keep_row, mask_ref, p_ref, u_ref, *faces):
    def snapshot(index):
        for strip in range(2):
            mask = jnp.broadcast_to(mask_ref[strip, pl.ds(index, 1), :], (8, WIDE))
            fast = mask * (1.0 / DT)

            def keep_rows(turn, carry, strip=strip, mask=mask, fast=fast):
                for extra in range(4):
                    at = turn * 4 + extra + 8 * strip
                    keep_row(index, at, (OWN + at) * sets, mask, fast)
                return carry

            lax.fori_loop(0, 2, keep_rows, 0)

    def advance(index, carry):
        step(2 * index, sets, unroll, p_ref, u_ref, *faces)
        step(2 * index + 1, sets, unroll, p_ref, u_ref, *faces)
        snapshot(index)
        return carry

    step(1, sets, unroll, p_ref, u_ref, *faces)
    snapshot(0)
    lax.fori_loop(1, SNAPS, advance, 0)


def in_order(side, sets, p_ref):
    shape = (WIDE, HALF)
    pick = one_hot(lax.broadcasted_iota(jnp.int32, shape, 1) == block_column(shape, 0))
    turn = row_major(8 * sets, inverse=True)
    for base in strip_bases(side)[:2]:
        cells = p_ref[pl.ds(base * sets, ROWS * sets)].reshape(ROWS * 8 * sets, WIDE)
        yield pick_columns(turn_rows(halves(cells), turn), pick).reshape(8 * sets, ROWS, HALF)


def sensor_kernel(
    side_ref, stiff_ref, dens_ref,
    keep_ref, give_ref, up_ref, dn_ref, far_keep_ref, far_give_ref,
    own_ref, other_ref, frames_ref, fx_ref, fy_ref, fw_ref, mk_ref, mask_ref,
    p_ref, u_ref, s_ref, m_ref, fs_ref,
):
    side = side_ref[0]
    strips = [keep_ref, give_ref.at[0:SENS_SLABS]]
    for ref in (up_ref, dn_ref):
        strips += [ref.at[0:SENS_SLABS], ref.at[SENS_SLABS:]]
    far = (far_keep_ref, far_give_ref)

    def materials(ids, base):
        stiff = jnp.zeros_like(ids)
        dens = jnp.zeros_like(ids)
        for region in range(REGIONS):
            here = ids == region + 1.0
            stiff = jnp.where(here, stiff_ref[region], stiff)
            dens = jnp.where(here, dens_ref[region], dens)
        inside = ids > 0.0
        rows = pl.ds(pl.multiple_of(base, 8), 8)
        s_ref[rows, :] = stiff
        m_ref[rows, :] = jnp.where(inside, (0.5 * DT * DT) / jnp.where(inside, dens, 1.0), 0.0)

    for ref, base in zip(strips, strip_bases(side)):
        materials(ref[ROWS], base)
    for ref, above in zip(far, (side, 1 - side)):
        materials(ref[FAR - 1], (ALL_ROWS - 8) * (1 - above))
    shape = (8, WIDE)
    tile = 4 * side + (block_column(shape, 1) >> 7)
    inside = block_column(shape, 1) < HALF
    spread = one_hot(inside & (lax.broadcasted_iota(jnp.int32, shape, 0) == tile))
    for ref, strip in ((keep_ref, side), (give_ref, 1 - side)):
        flags = ref[ROWS, :, 0:LANES].astype(jnp.bfloat16)
        masks = lax.dot_general(flags, spread, (((0,), (0,)), ((), ())), **FAST)
        mask_ref[strip] = masks[FLAG_LANE:LANES]

    def coefficients(turn, carry):
        for extra in range(9):
            row = 1 + turn * 9 + extra
            centre = jnp.broadcast_to(s_ref[pl.ds(row, 1), :], (8, WIDE))
            upper = jnp.broadcast_to(s_ref[pl.ds(row - 1, 1), :], (8, WIDE))
            fx_ref[row] = centre + upper
            fy_ref[row] = centre + after(centre)
            fw_ref[row] = centre[:, :LANES] + pltpu.roll(centre[:, WIDE - LANES :], 1, 1)
            mk_ref[row] = jnp.broadcast_to(m_ref[pl.ds(row, 1), :], (8, WIDE))
        return carry

    lax.fori_loop(0, (ALL_ROWS - 1) // 9, coefficients, 0)
    fill(side, strips, far, 1, ACT_SETS, p_ref, u_ref, mk_ref)

    def keep_row(index, at, spot, mask, fast):
        rows = pl.ds(pl.multiple_of(index * SENS, SENS), SENS)
        fs_ref[at, rows, 0:WIDE] = p_ref[spot] * mask
        fs_ref[at, rows, WIDE : 2 * WIDE] = u_ref[spot] * fast

    march(1, 8, keep_row, mask_ref, p_ref, u_ref, fx_ref, fy_ref, fw_ref, mk_ref)

    def narrow(row, carry):
        frames_ref[row] = fs_ref[row].astype(jnp.bfloat16)
        return carry

    lax.fori_loop(0, CENTRE_ROWS, narrow, 0)
    for out_ref, cells in zip((own_ref, other_ref), in_order(side, 1, p_ref)):
        out_ref[...] = cells


def actuator_kernel(
    side_ref, place_ref,
    keep_ref, give_ref, up_ref, dn_ref, far_keep_ref, far_give_ref,
    own_sens_ref, other_sens_ref, frames_ref, fx_ref, fy_ref, fw_ref, mk_ref, mask_ref,
    own_ref, other_ref, piece_0_ref, piece_1_ref, piece_2_ref, piece_3_ref,
    p_ref, u_ref, fa_ref, acc_ref,
):
    side = side_ref[0]
    strips = [keep_ref, give_ref.at[SENS_SLABS:]]
    for ref in (up_ref, dn_ref):
        strips += [ref.at[0:ACT_SLABS], ref.at[ACT_SLABS:]]
    fill(side, strips, (far_keep_ref, far_give_ref), ACT_SETS, 0, p_ref, u_ref, mk_ref)

    def keep_row(index, at, spot, mask, fast):
        rows = pl.ds(pl.multiple_of(index * ACT, ACT), ACT)
        place = jnp.concatenate([p_ref[spot] * mask, p_ref[spot + 1] * mask], axis=0)
        speed = jnp.concatenate([u_ref[spot] * fast, u_ref[spot + 1] * fast], axis=0)
        fa_ref[at, rows, 0:WIDE] = place.astype(jnp.bfloat16)
        fa_ref[at, rows, WIDE : 2 * WIDE] = speed.astype(jnp.bfloat16)

    march(ACT_SETS, 6, keep_row, mask_ref, p_ref, u_ref, fx_ref, fy_ref, fw_ref, mk_ref)

    def gram(turn, total):
        for extra in range(4):
            row = 4 * turn + extra
            total = total + lax.dot_general(fa_ref[row], frames_ref[row], (((1,), (1,)), ((), ())), **FAST)
        return total

    total = lax.fori_loop(0, CENTRE_ROWS // 4, gram, jnp.zeros((ACT * SNAPS, SENS * SNAPS), jnp.float32))
    shape = (ACT * SNAPS, ACT * SNAPS)
    old = lax.broadcasted_iota(jnp.int32, shape, 1)
    new = lax.broadcasted_iota(jnp.int32, shape, 0)
    turn = jnp.where(new == (old & (ACT - 1)) * SNAPS + (old >> 4), 1.0, 0.0)
    shape = (SENS * SNAPS, SENS * SNAPS)
    old = lax.broadcasted_iota(jnp.int32, shape, 0)
    new = lax.broadcasted_iota(jnp.int32, shape, 1)
    turn_back = jnp.where(new == (old & (SENS - 1)) * SNAPS + (old >> 3), 1.0, 0.0)
    turned = lax.dot_general(turn, total, MATMUL, **EXACT)
    acc_ref[...] = lax.dot_general(turned, turn_back, MATMUL, **EXACT) * (1.0 / math.sqrt(CELLS))
    place = place_ref[0]
    for hop, out_ref in enumerate((piece_0_ref, piece_1_ref, piece_2_ref, piece_3_ref)):
        out_ref[...] = acc_ref[pl.ds(pl.multiple_of(((place + hop) & 3) * SHARE, 8), SHARE), :]
    for out_ref, cells, sens_ref in zip(
        (own_ref, other_ref), in_order(side, ACT_SETS, p_ref), (own_sens_ref, other_sens_ref)
    ):
        out_ref[0:ACT] = cells
        out_ref[ACT:RESP] = sens_ref[...]


def array(*shape, dtype=jnp.float32):
    return jax.ShapeDtypeStruct(shape, dtype)


def scratch(*shape, dtype=jnp.float32):
    return pltpu.VMEM(shape, dtype)


def call(kernel, scalars, operands, out_shape, scratch_shapes, mebibytes):
    vmem = pl.BlockSpec(memory_space=pltpu.VMEM)
    smem = pl.BlockSpec(memory_space=pltpu.SMEM)
    return pl.pallas_call(
        kernel,
        out_shape=out_shape,
        in_specs=[smem] * len(scalars) + [vmem] * len(operands),
        out_specs=(vmem,) * len(out_shape),
        scratch_shapes=scratch_shapes,
        compiler_params=grant(mebibytes),
    )(*scalars, *operands)


def sensor_block(scalars, operands):
    face = array(ALL_ROWS, 8, WIDE)
    part = array(SENS, ROWS, HALF)
    return call(
        sensor_kernel, scalars, operands,
        (
            part, part, array(CENTRE_ROWS, SENS * SNAPS, 2 * WIDE, dtype=jnp.bfloat16),
            face, face, array(ALL_ROWS, 8, LANES), face, array(2, LANES - FLAG_LANE, WIDE),
        ),
        [
            scratch(ALL_ROWS, 8, WIDE), scratch(ALL_ROWS, 8, WIDE), scratch(ALL_ROWS, WIDE), scratch(ALL_ROWS, WIDE),
            scratch(CENTRE_ROWS, SENS * SNAPS, 2 * WIDE),
        ],
        28,
    )


def actuator_block(scalars, operands):
    part = array(RESP, ROWS, HALF)
    state = scratch(ALL_ROWS * ACT_SETS, 8, WIDE)
    return call(
        actuator_kernel, scalars, operands,
        (part, part) + (array(SHARE, SENS * SNAPS),) * 4,
        [
            state, state,
            scratch(CENTRE_ROWS, ACT * SNAPS, 2 * WIDE, dtype=jnp.bfloat16),
            scratch(ACT * SNAPS, SENS * SNAPS),
        ],
        36,
    )


def along_dom(cells, distance):
    count = lax.axis_size("dom")
    return lax.ppermute(cells, "dom", [(i, i + distance) for i in range(count) if 0 <= i + distance < count])


def outward(cells, distance):
    count = lax.axis_size("dom")
    pairs = [(i, i + distance if i % 2 else i - distance) for i in range(count)]
    return lax.ppermute(cells, "dom", [(i, j) for i, j in pairs if 0 <= j < count])


def grant(mebibytes):
    return pltpu.CompilerParams(vmem_limit_bytes=mebibytes << 20)


def swap(cells, bit):
    count = lax.axis_size("dom")
    return lax.ppermute(cells, "dom", [(i, i ^ bit) for i in range(count)])


def body(actuator_fields, sensor_fields, region_ids, stiffness_table, density_table, supported):
    side = lax.axis_index("dom") % 2
    side_word = side.astype(jnp.int32).reshape(1)
    place_word = lax.axis_index("sec").astype(jnp.int32).reshape(1)
    sections = lax.axis_size("sec")
    right_edge, left_edge = edges(actuator_fields, sensor_fields, region_ids)
    left = lax.ppermute(right_edge, "sec", [(i, i + 1) for i in range(sections - 1)])
    right = lax.ppermute(left_edge, "sec", [(i + 1, i) for i in range(sections - 1)])
    flags = jnp.transpose(supported, (1, 2, 0)).reshape(-1, SNAPS)

    vmem = pl.BlockSpec(memory_space=pltpu.VMEM)
    smem = pl.BlockSpec(memory_space=pltpu.SMEM)
    block = jax.ShapeDtypeStruct((SLABS, 8, WIDE), jnp.float32)
    first, second = pl.pallas_call(
        main_kernel, out_shape=(block, block), in_specs=[vmem] * 4, out_specs=(vmem, vmem), compiler_params=grant(16)
    )(actuator_fields, sensor_fields, region_ids, flags)
    far = array(FAR, 8, WIDE)
    outs = (array(SENS_SLABS, 8, WIDE), array(ACT_SLABS, 8, WIDE), block, far, far)
    keep_s, keep_a, give, far_keep, far_give = call(halo_kernel, (side_word,), (first, second, left, right), outs, [], 16)

    far_keep = outward(far_keep, 4)
    got = swap(give, 1)
    far_give = outward(far_give, 3)
    both_s = jnp.concatenate([keep_s, got[:SENS_SLABS]], 0)
    up_s = along_dom(both_s, 2)
    dn_s = along_dom(both_s, -2)
    both_a = jnp.concatenate([keep_a, got[SENS_SLABS:]], 0)
    up_a = along_dom(both_a, 2)
    dn_a = along_dom(both_a, -2)
    far = (far_keep, far_give)
    sensor = sensor_block((side_word, stiffness_table, density_table), (keep_s, got, up_s, dn_s) + far)
    own, other, *pieces = actuator_block((side_word, place_word), (keep_a, got, up_a, dn_a) + far + tuple(sensor))
    total = pieces[0]
    for hop in range(1, sections):
        total = total + lax.ppermute(pieces[hop], "sec", [(i, (i + hop) % sections) for i in range(sections)])
    other, total = lax.optimization_barrier((other, total))
    back = swap(other, 1)
    position = jnp.where(
        side == 0, jnp.concatenate([own, back], 2), jnp.concatenate([back, own], 2)
    )
    for bits in (4, 12, 16, 48):
        total = total + swap(total, bits)
    position, total = lax.optimization_barrier((position, total))
    total = total + sum(swap(total, bits) for bits in (1, 2, 3))
    return (position, total)


def solution(mesh):
    in_specs = (
        P(None, "dom", "sec"),
        P(None, "dom", "sec"),
        P("dom", "sec"),
        P(),
        P(),
        P(None, "dom", "sec"),
    )
    out_specs = (P(None, "dom", "sec"), P("sec", None))
    return jax.shard_map(body, mesh=mesh, in_specs=in_specs, out_specs=out_specs, check_vma=False)
```

```python
import math

import jax
import jax.numpy as jnp
from jax import lax
from jax.experimental import pallas as pl
from jax.experimental.pallas import tpu as pltpu
from jax.sharding import PartitionSpec as P


ROWS = 8
COLS = 1024
HALF = 512
LANES = 128
TILES = 5
WIDE = TILES * LANES
HALO = 20
ACT = 16
SENS = 8
RESP = ACT + SENS
SETS = RESP // 8
SNAPS = 10
STEPS = 20
REGIONS = 16
SLABS = ROWS * SETS + 1
NEAR = 3
FAR = NEAR * SETS + 1
OWN = 24
SHARE = 40
CELLS = 512 * 4096
FLAG_LANE = 112
ACT_SETS = ACT // 8
CENTRE_ROWS = 2 * ROWS
SENS_SLABS = ROWS + 1
ACT_SLABS = ROWS * ACT_SETS
ALL_ROWS = 64
ROOM = 80
DT = 0.35


def block_column(shape, dim):
    spot = lax.broadcasted_iota(jnp.int32, shape, dim)
    return (spot & (LANES - 1)) * TILES + (spot >> 7)


MATMUL = (((1,), (0,)), ((), ()))
FAST = dict(preferred_element_type=jnp.float32)
EXACT = dict(precision=lax.Precision.HIGHEST, preferred_element_type=jnp.float32)


def one_hot(hit):
    return jnp.where(hit, 1.0, 0.0).astype(jnp.bfloat16)


def halves(cells):
    high = cells.astype(jnp.bfloat16)
    return high, (cells - high.astype(jnp.float32)).astype(jnp.bfloat16)


def pick_columns(parts, pick):
    return sum(lax.dot_general(part, pick, MATMUL, **FAST) for part in parts)


def turn_rows(parts, turn):
    return [lax.dot_general(turn, part, MATMUL, **FAST).astype(jnp.bfloat16) for part in parts]


def row_major(count=RESP, inverse=False):
    shape = (ROWS * count, ROWS * count)
    old = lax.broadcasted_iota(jnp.int32, shape, 0 if inverse else 1)
    new = lax.broadcasted_iota(jnp.int32, shape, 1 if inverse else 0)
    return one_hot(new == (old & (ROWS - 1)) * count + (old >> 3))


def edge_kernel(*refs):
    for act_ref, sens_ref, ids_ref, out_ref in (refs[0:3] + refs[6:7], refs[3:6] + refs[7:8]):
        out_ref[0:ACT] = act_ref[...]
        out_ref[ACT:RESP] = sens_ref[...]
        out_ref[RESP] = ids_ref[...].astype(jnp.float32) + 1.0


def edges(actuator_fields, sensor_fields, region_ids):
    def blocks(column):
        return [
            pl.BlockSpec((ACT, ROWS, LANES), lambda i, c=column: (0, 0, c)),
            pl.BlockSpec((SENS, ROWS, LANES), lambda i, c=column: (0, 0, c)),
            pl.BlockSpec((ROWS, LANES), lambda i, c=column: (0, c)),
        ]

    out = jax.ShapeDtypeStruct((RESP + 1, ROWS, LANES), jnp.float32)
    whole = pl.BlockSpec((RESP + 1, ROWS, LANES), lambda i: (0, 0, 0))
    fields = (actuator_fields, sensor_fields, region_ids)
    return pl.pallas_call(
        edge_kernel,
        grid=(1,),
        out_shape=(out, out),
        in_specs=blocks(COLS // LANES - 1) + blocks(0),
        out_specs=(whole, whole),
    )(*fields, *fields)


def main_kernel(act_ref, sens_ref, ids_ref, sup_ref, first_ref, second_ref):
    turn = row_major()
    cells = jnp.concatenate(
        [act_ref[...].reshape(ACT * ROWS, COLS), sens_ref[...].reshape(SENS * ROWS, COLS)], axis=0
    )
    parts = turn_rows(halves(cells), turn)
    ids = (ids_ref[...].astype(jnp.float32) + 1.0).astype(jnp.bfloat16)
    shape = (WIDE, WIDE)
    column = block_column(shape, 1)
    source = lax.broadcasted_iota(jnp.int32, shape, 0)
    inner = column < HALF + HALO
    outer = column >= WIDE - HALO
    for out_ref, begin, wanted in (
        (first_ref, 0, jnp.where(inner, column, -1)),
        (second_ref, COLS - WIDE, jnp.where(column < HALF, column + LANES, jnp.where(outer, column - HALF, -1))),
    ):
        pick = one_hot(source == wanted)
        cut = slice(begin, begin + WIDE)
        out_ref[0 : SLABS - 1] = pick_columns([part[:, cut] for part in parts], pick).reshape(SLABS - 1, 8, WIDE)
        out_ref[SLABS - 1] = pick_columns([ids[:, cut]], pick)
        out_ref[SLABS - 1, :, FLAG_LANE : FLAG_LANE + SNAPS] = sup_ref[...].astype(jnp.float32)


def halo_kernel(side_ref, first_ref, second_ref, left_ref, right_ref, *out_refs):
    turn = row_major()
    shape = (LANES, WIDE)
    column = block_column(shape, 1)
    source = lax.broadcasted_iota(jnp.int32, shape, 0)
    blocks = []
    for in_ref, edge_ref, hit in (
        (first_ref, left_ref, (column >= WIDE - HALO) & (source == column - HALF)),
        (second_ref, right_ref, (column >= HALF) & (column < HALF + HALO) & (source == column - HALF)),
    ):
        pick = one_hot(hit)
        parts = turn_rows(halves(edge_ref[0:RESP].reshape(RESP * ROWS, LANES)), turn)
        fields = in_ref[0 : SLABS - 1] + pick_columns(parts, pick).reshape(SLABS - 1, 8, WIDE)
        ids = in_ref[SLABS - 1] + pick_columns([edge_ref[RESP].astype(jnp.bfloat16)], pick)
        blocks.append((fields, ids))
    low_side = side_ref[0] == 0
    (fields_0, ids_0), (fields_1, ids_1) = blocks
    near = NEAR * SETS
    keep_s_ref, keep_a_ref, far_keep_ref, give_s_ref, give_a_ref, far_give_ref = out_refs
    for sens_ref, act_ref, far_ref, fields, ids in (
        (keep_s_ref, keep_a_ref, far_keep_ref, jnp.where(low_side, fields_0, fields_1), jnp.where(low_side, ids_0, ids_1)),
        (
            give_s_ref, give_a_ref, far_give_ref,
            jnp.where(low_side, fields_1, fields_0), jnp.where(low_side, ids_1, ids_0),
        ),
    ):
        grid = fields.reshape(ROWS, SETS, 8, WIDE)
        act_ref[...] = grid[:, :ACT_SETS].reshape(ACT_SLABS, 8, WIDE)
        sens_ref[0:ROWS] = grid[:, ACT_SETS]
        sens_ref[ROWS] = ids
        far_ref[0:near] = jnp.where(low_side, fields[:near], fields[SLABS - 1 - near :])
        far_ref[near] = ids


def after(cells):
    return jnp.concatenate([cells[:, LANES:], pltpu.roll(cells[:, :LANES], LANES - 1, 1)], axis=1)


def strip_bases(side):
    return [OWN + shift + spot for shift in (0, -16, 16) for spot in (8 * side, 8 - 8 * side)]


def fill(side, strips, far, sets, offset, p_ref, u_ref, mk_ref):
    def place(slab, row, spot):
        begin = slab * (mk_ref[row] * (DT / (0.5 * DT * DT)))
        u_ref[spot] = begin
        p_ref[spot] = begin

    for ref, base in zip(strips, strip_bases(side)):
        def fill_row(row, carry, ref=ref, base=base):
            for index in range(sets):
                place(ref[row * sets + index], base + row, (base + row) * sets + index)
            return carry

        lax.fori_loop(0, ROWS, fill_row, 0)
    for ref, above in zip(far, (side, 1 - side)):
        base = above * (8 - NEAR) + (ALL_ROWS - 8) * (1 - above)
        for row in range(NEAR):
            for index in range(sets):
                place(ref[row * SETS + offset + index], base + row, (base + row) * sets + index)


def step(count, sets, unroll, p_ref, u_ref, fx_ref, fy_ref, fw_ref, mk_ref):
    first = OWN - STEPS + 1 + count
    rows = CENTRE_ROWS + 2 * (STEPS - 1) - 2 * count

    def start(index):
        centre = p_ref[first * sets + index]
        north = fx_ref[first] * (centre - p_ref[(first - 1) * sets + index])
        return centre, north

    def one(row, carry):
        face = fx_ref[row + 1]
        along = fy_ref[row]
        back = fw_ref[row]
        mass = mk_ref[row]
        done = []
        for index, (centre, north) in enumerate(carry):
            spot = row * sets + index
            below = p_ref[spot + sets]
            south = face * (below - centre)
            east = along * (after(centre) - centre)
            first_west = back * (centre[:, :LANES] - pltpu.roll(centre[:, WIDE - LANES :], 1, 1))
            west = jnp.concatenate([first_west, east[:, : WIDE - LANES]], axis=1)
            speed = u_ref[spot] + mass * ((south - north) + (east - west))
            u_ref[spot] = speed
            p_ref[spot] = centre + speed
            done.append((below, south))
        return tuple(done)

    def several(turn, carry):
        row = first + unroll * turn
        for extra in range(unroll):
            carry = one(row + extra, carry)
        return carry

    lax.fori_loop(0, (rows + unroll - 1) // unroll, several, tuple(start(index) for index in range(sets)))


def march(sets, unroll, keep_row, mask_ref, p_ref, u_ref, *faces):
    def snapshot(index):
        for strip in range(2):
            mask = jnp.broadcast_to(mask_ref[strip, pl.ds(index, 1), :], (8, WIDE))
            fast = mask * (1.0 / DT)

            def keep_rows(turn, carry, strip=strip, mask=mask, fast=fast):
                for extra in range(4):
                    at = turn * 4 + extra + 8 * strip
                    keep_row(index, at, (OWN + at) * sets, mask, fast)
                return carry

            lax.fori_loop(0, 2, keep_rows, 0)

    def advance(index, carry):
        step(2 * index, sets, unroll, p_ref, u_ref, *faces)
        step(2 * index + 1, sets, unroll, p_ref, u_ref, *faces)
        snapshot(index)
        return carry

    step(1, sets, unroll, p_ref, u_ref, *faces)
    snapshot(0)
    lax.fori_loop(1, SNAPS, advance, 0)


def in_order(side, sets, p_ref):
    shape = (WIDE, HALF)
    pick = one_hot(lax.broadcasted_iota(jnp.int32, shape, 1) == block_column(shape, 0))
    turn = row_major(8 * sets, inverse=True)
    for base in strip_bases(side)[:2]:
        cells = p_ref[pl.ds(base * sets, ROWS * sets)].reshape(ROWS * 8 * sets, WIDE)
        yield pick_columns(turn_rows(halves(cells), turn), pick).reshape(8 * sets, ROWS, HALF)


def sensor_kernel(
    side_ref, stiff_ref, dens_ref,
    keep_ref, give_ref, up_ref, dn_ref, far_keep_ref, far_give_ref,
    own_ref, other_ref, frames_ref, fx_ref, fy_ref, fw_ref, mk_ref, mask_ref,
    p_ref, u_ref, s_ref, m_ref, fs_ref,
):
    side = side_ref[0]
    strips = [keep_ref, give_ref]
    for ref in (up_ref, dn_ref):
        strips += [ref.at[0:SENS_SLABS], ref.at[SENS_SLABS:]]
    far = (far_keep_ref, far_give_ref)

    def materials(ids, base):
        stiff = jnp.zeros_like(ids)
        dens = jnp.zeros_like(ids)
        for region in range(REGIONS):
            here = ids == region + 1.0
            stiff = jnp.where(here, stiff_ref[region], stiff)
            dens = jnp.where(here, dens_ref[region], dens)
        inside = ids > 0.0
        rows = pl.ds(pl.multiple_of(base, 8), 8)
        s_ref[rows, :] = stiff
        m_ref[rows, :] = jnp.where(inside, (0.5 * DT * DT) / jnp.where(inside, dens, 1.0), 0.0)

    for ref, base in zip(strips, strip_bases(side)):
        materials(ref[ROWS], base)
    for ref, above in zip(far, (side, 1 - side)):
        materials(ref[FAR - 1], (ALL_ROWS - 8) * (1 - above))
    shape = (8, WIDE)
    tile = 4 * side + (block_column(shape, 1) >> 7)
    inside = block_column(shape, 1) < HALF
    spread = one_hot(inside & (lax.broadcasted_iota(jnp.int32, shape, 0) == tile))
    for ref, strip in ((keep_ref, side), (give_ref, 1 - side)):
        flags = ref[ROWS, :, 0:LANES].astype(jnp.bfloat16)
        masks = lax.dot_general(flags, spread, (((0,), (0,)), ((), ())), **FAST)
        mask_ref[strip] = masks[FLAG_LANE:LANES]

    def coefficients(turn, carry):
        for extra in range(9):
            row = 1 + turn * 9 + extra
            centre = jnp.broadcast_to(s_ref[pl.ds(row, 1), :], (8, WIDE))
            upper = jnp.broadcast_to(s_ref[pl.ds(row - 1, 1), :], (8, WIDE))
            fx_ref[row] = centre + upper
            fy_ref[row] = centre + after(centre)
            fw_ref[row] = centre[:, :LANES] + pltpu.roll(centre[:, WIDE - LANES :], 1, 1)
            mk_ref[row] = jnp.broadcast_to(m_ref[pl.ds(row, 1), :], (8, WIDE))
        return carry

    lax.fori_loop(0, (ALL_ROWS - 1) // 9, coefficients, 0)
    fill(side, strips, far, 1, ACT_SETS, p_ref, u_ref, mk_ref)

    def keep_row(index, at, spot, mask, fast):
        rows = pl.ds(pl.multiple_of(index * SENS, SENS), SENS)
        fs_ref[at, rows, 0:WIDE] = p_ref[spot] * mask
        fs_ref[at, rows, WIDE : 2 * WIDE] = u_ref[spot] * fast

    march(1, 16, keep_row, mask_ref, p_ref, u_ref, fx_ref, fy_ref, fw_ref, mk_ref)

    def narrow(row, carry):
        frames_ref[row] = fs_ref[row].astype(jnp.bfloat16)
        return carry

    lax.fori_loop(0, CENTRE_ROWS, narrow, 0)
    for out_ref, cells in zip((own_ref, other_ref), in_order(side, 1, p_ref)):
        out_ref[...] = cells


def actuator_kernel(
    side_ref, place_ref,
    keep_ref, give_ref, up_ref, dn_ref, far_keep_ref, far_give_ref,
    own_sens_ref, other_sens_ref, frames_ref, fx_ref, fy_ref, fw_ref, mk_ref, mask_ref,
    own_ref, other_ref, piece_0_ref, piece_1_ref, piece_2_ref, piece_3_ref,
    p_ref, u_ref, fa_ref, acc_ref,
):
    side = side_ref[0]
    strips = [keep_ref, give_ref]
    for ref in (up_ref, dn_ref):
        strips += [ref.at[0:ACT_SLABS], ref.at[ACT_SLABS:]]
    fill(side, strips, (far_keep_ref, far_give_ref), ACT_SETS, 0, p_ref, u_ref, mk_ref)

    def keep_row(index, at, spot, mask, fast):
        rows = pl.ds(pl.multiple_of(index * ACT, ACT), ACT)
        place = jnp.concatenate([p_ref[spot] * mask, p_ref[spot + 1] * mask], axis=0)
        speed = jnp.concatenate([u_ref[spot] * fast, u_ref[spot + 1] * fast], axis=0)
        fa_ref[at, rows, 0:WIDE] = place.astype(jnp.bfloat16)
        fa_ref[at, rows, WIDE : 2 * WIDE] = speed.astype(jnp.bfloat16)

    march(ACT_SETS, 6, keep_row, mask_ref, p_ref, u_ref, fx_ref, fy_ref, fw_ref, mk_ref)

    def gram(turn, total):
        for extra in range(4):
            row = 4 * turn + extra
            total = total + lax.dot_general(fa_ref[row], frames_ref[row], (((1,), (1,)), ((), ())), **FAST)
        return total

    total = lax.fori_loop(0, CENTRE_ROWS // 4, gram, jnp.zeros((ACT * SNAPS, SENS * SNAPS), jnp.float32))
    shape = (ACT * SNAPS, ACT * SNAPS)
    old = lax.broadcasted_iota(jnp.int32, shape, 1)
    new = lax.broadcasted_iota(jnp.int32, shape, 0)
    turn = jnp.where(new == (old & (ACT - 1)) * SNAPS + (old >> 4), 1.0, 0.0)
    shape = (SENS * SNAPS, SENS * SNAPS)
    old = lax.broadcasted_iota(jnp.int32, shape, 0)
    new = lax.broadcasted_iota(jnp.int32, shape, 1)
    turn_back = jnp.where(new == (old & (SENS - 1)) * SNAPS + (old >> 3), 1.0, 0.0)
    turned = lax.dot_general(turn, total, MATMUL, **EXACT)
    acc_ref[...] = lax.dot_general(turned, turn_back, MATMUL, **EXACT) * (1.0 / math.sqrt(CELLS))
    place = place_ref[0]
    for hop, out_ref in enumerate((piece_0_ref, piece_1_ref, piece_2_ref, piece_3_ref)):
        out_ref[...] = acc_ref[pl.ds(pl.multiple_of(((place + hop) & 3) * SHARE, 8), SHARE), :]
    for out_ref, cells, sens_ref in zip(
        (own_ref, other_ref), in_order(side, ACT_SETS, p_ref), (own_sens_ref, other_sens_ref)
    ):
        out_ref[0:ACT] = cells
        out_ref[ACT:RESP] = sens_ref[...]


def array(*shape, dtype=jnp.float32):
    return jax.ShapeDtypeStruct(shape, dtype)


def scratch(*shape, dtype=jnp.float32):
    return pltpu.VMEM(shape, dtype)


def call(kernel, scalars, operands, out_shape, scratch_shapes, mebibytes):
    vmem = pl.BlockSpec(memory_space=pltpu.VMEM)
    smem = pl.BlockSpec(memory_space=pltpu.SMEM)
    return pl.pallas_call(
        kernel,
        out_shape=out_shape,
        in_specs=[smem] * len(scalars) + [vmem] * len(operands),
        out_specs=(vmem,) * len(out_shape),
        scratch_shapes=scratch_shapes,
        compiler_params=grant(mebibytes),
    )(*scalars, *operands)


def join_kernel(first_ref, second_ref, out_ref):
    count = first_ref.shape[0]
    out_ref[0:count] = first_ref[...]
    out_ref[count:] = second_ref[...]


def joined(first, second):
    count = first.shape[0]
    return call(join_kernel, (), (first, second), (array(2 * count, 8, WIDE),), [], 8)[0]


def sensor_block(scalars, operands):
    face = array(ROOM, 8, WIDE)
    part = array(SENS, ROWS, HALF)
    return call(
        sensor_kernel, scalars, operands,
        (
            part, part, array(CENTRE_ROWS, SENS * SNAPS, 2 * WIDE, dtype=jnp.bfloat16),
            face, face, array(ROOM, 8, LANES), face, array(2, LANES - FLAG_LANE, WIDE),
        ),
        [
            scratch(ROOM, 8, WIDE), scratch(ROOM, 8, WIDE), scratch(ALL_ROWS, WIDE), scratch(ALL_ROWS, WIDE),
            scratch(CENTRE_ROWS, SENS * SNAPS, 2 * WIDE),
        ],
        28,
    )


def actuator_block(scalars, operands):
    part = array(RESP, ROWS, HALF)
    state = scratch(ROOM * ACT_SETS, 8, WIDE)
    return call(
        actuator_kernel, scalars, operands,
        (part, part) + (array(SHARE, SENS * SNAPS),) * 4,
        [
            state, state,
            scratch(CENTRE_ROWS, ACT * SNAPS, 2 * WIDE, dtype=jnp.bfloat16),
            scratch(ACT * SNAPS, SENS * SNAPS),
        ],
        36,
    )


def along_dom(cells, distance):
    count = lax.axis_size("dom")
    return lax.ppermute(cells, "dom", [(i, i + distance) for i in range(count) if 0 <= i + distance < count])


def outward(cells, distance):
    count = lax.axis_size("dom")
    pairs = [(i, i + distance if i % 2 else i - distance) for i in range(count)]
    return lax.ppermute(cells, "dom", [(i, j) for i, j in pairs if 0 <= j < count])


def grant(mebibytes):
    return pltpu.CompilerParams(vmem_limit_bytes=mebibytes << 20)


def swap(cells, bit):
    count = lax.axis_size("dom")
    return lax.ppermute(cells, "dom", [(i, i ^ bit) for i in range(count)])


def body(actuator_fields, sensor_fields, region_ids, stiffness_table, density_table, supported):
    side = lax.axis_index("dom") % 2
    side_word = side.astype(jnp.int32).reshape(1)
    place_word = lax.axis_index("sec").astype(jnp.int32).reshape(1)
    sections = lax.axis_size("sec")
    right_edge, left_edge = edges(actuator_fields, sensor_fields, region_ids)
    left = lax.ppermute(right_edge, "sec", [(i, i + 1) for i in range(sections - 1)])
    right = lax.ppermute(left_edge, "sec", [(i + 1, i) for i in range(sections - 1)])
    flags = jnp.transpose(supported, (1, 2, 0)).reshape(-1, SNAPS)

    vmem = pl.BlockSpec(memory_space=pltpu.VMEM)
    smem = pl.BlockSpec(memory_space=pltpu.SMEM)
    block = jax.ShapeDtypeStruct((SLABS, 8, WIDE), jnp.float32)
    first, second = pl.pallas_call(
        main_kernel, out_shape=(block, block), in_specs=[vmem] * 4, out_specs=(vmem, vmem), compiler_params=grant(16)
    )(actuator_fields, sensor_fields, region_ids, flags)
    far = array(FAR, 8, WIDE)
    outs = (array(SENS_SLABS, 8, WIDE), array(ACT_SLABS, 8, WIDE), far)
    keep_s, keep_a, far_keep, give_s, give_a, far_give = call(
        halo_kernel, (side_word,), (first, second, left, right), outs + outs, [], 16
    )

    got_s = swap(give_s, 1)
    got_a = swap(give_a, 1)
    far_keep = outward(far_keep, 4)
    far_give = outward(far_give, 3)
    both_s = joined(keep_s, got_s)
    up_s = along_dom(both_s, 2)
    dn_s = along_dom(both_s, -2)
    both_a = joined(keep_a, got_a)
    up_a = along_dom(both_a, 2)
    dn_a = along_dom(both_a, -2)
    far = (far_keep, far_give)
    sensor = sensor_block((side_word, stiffness_table, density_table), (keep_s, got_s, up_s, dn_s) + far)
    own, other, *pieces = actuator_block((side_word, place_word), (keep_a, got_a, up_a, dn_a) + far + tuple(sensor))
    total = pieces[0]
    for hop in range(1, sections):
        total = total + lax.ppermute(pieces[hop], "sec", [(i, (i + hop) % sections) for i in range(sections)])
    other, total = lax.optimization_barrier((other, total))
    back = swap(other, 1)
    for bits in (4, 12, 16, 48):
        total = total + swap(total, bits)
    position = jnp.where(side == 0, jnp.concatenate([own, back], 2), jnp.concatenate([back, own], 2))
    total = total + sum(swap(total, bits) for bits in (1, 2, 3))
    return (position, total)


def solution(mesh):
    in_specs = (
        P(None, "dom", "sec"),
        P(None, "dom", "sec"),
        P("dom", "sec"),
        P(),
        P(),
        P(None, "dom", "sec"),
    )
    out_specs = (P(None, "dom", "sec"), P("sec", None))
    return jax.shard_map(body, mesh=mesh, in_specs=in_specs, out_specs=out_specs, check_vma=False)
```

```python
import math

import jax
import jax.numpy as jnp
from jax import lax
from jax.experimental import pallas as pl
from jax.experimental.pallas import tpu as pltpu
from jax.sharding import PartitionSpec as P


ROWS = 8
COLS = 1024
HALF = 512
LANES = 128
TILES = 5
WIDE = TILES * LANES
HALO = 20
ACT = 16
SENS = 8
RESP = ACT + SENS
SETS = RESP // 8
SNAPS = 10
STEPS = 20
REGIONS = 16
SLABS = ROWS * SETS + 1
NEAR = 3
FAR = NEAR * SETS + 1
OWN = 24
SHARE = 40
CELLS = 512 * 4096
FLAG_LANE = 112
ACT_SETS = ACT // 8
CENTRE_ROWS = 2 * ROWS
SENS_SLABS = ROWS + 1
ACT_SLABS = ROWS * ACT_SETS
ALL_ROWS = 64
ROOM = 80
DT = 0.35


def block_column(shape, dim):
    spot = lax.broadcasted_iota(jnp.int32, shape, dim)
    return (spot & (LANES - 1)) * TILES + (spot >> 7)


MATMUL = (((1,), (0,)), ((), ()))
FAST = dict(preferred_element_type=jnp.float32)
EXACT = dict(precision=lax.Precision.HIGHEST, preferred_element_type=jnp.float32)


def one_hot(hit):
    return jnp.where(hit, 1.0, 0.0).astype(jnp.bfloat16)


def halves(cells):
    high = cells.astype(jnp.bfloat16)
    return high, (cells - high.astype(jnp.float32)).astype(jnp.bfloat16)


def pick_columns(parts, pick):
    return sum(lax.dot_general(part, pick, MATMUL, **FAST) for part in parts)


def turn_rows(parts, turn):
    return [lax.dot_general(turn, part, MATMUL, **FAST).astype(jnp.bfloat16) for part in parts]


def row_major(count=RESP, inverse=False):
    shape = (ROWS * count, ROWS * count)
    old = lax.broadcasted_iota(jnp.int32, shape, 0 if inverse else 1)
    new = lax.broadcasted_iota(jnp.int32, shape, 1 if inverse else 0)
    return one_hot(new == (old & (ROWS - 1)) * count + (old >> 3))


def edge_kernel(*refs):
    for act_ref, sens_ref, ids_ref, out_ref in (refs[0:3] + refs[6:7], refs[3:6] + refs[7:8]):
        out_ref[0:ACT] = act_ref[...]
        out_ref[ACT:RESP] = sens_ref[...]
        out_ref[RESP] = ids_ref[...].astype(jnp.float32) + 1.0


def edges(actuator_fields, sensor_fields, region_ids):
    def blocks(column):
        return [
            pl.BlockSpec((ACT, ROWS, LANES), lambda i, c=column: (0, 0, c)),
            pl.BlockSpec((SENS, ROWS, LANES), lambda i, c=column: (0, 0, c)),
            pl.BlockSpec((ROWS, LANES), lambda i, c=column: (0, c)),
        ]

    out = jax.ShapeDtypeStruct((RESP + 1, ROWS, LANES), jnp.float32)
    whole = pl.BlockSpec((RESP + 1, ROWS, LANES), lambda i: (0, 0, 0))
    fields = (actuator_fields, sensor_fields, region_ids)
    return pl.pallas_call(
        edge_kernel,
        grid=(1,),
        out_shape=(out, out),
        in_specs=blocks(COLS // LANES - 1) + blocks(0),
        out_specs=(whole, whole),
    )(*fields, *fields)


def main_kernel(act_ref, sens_ref, ids_ref, sup_ref, first_ref, second_ref):
    turn = row_major()
    cells = jnp.concatenate(
        [act_ref[...].reshape(ACT * ROWS, COLS), sens_ref[...].reshape(SENS * ROWS, COLS)], axis=0
    )
    parts = turn_rows(halves(cells), turn)
    ids = (ids_ref[...].astype(jnp.float32) + 1.0).astype(jnp.bfloat16)
    shape = (WIDE, WIDE)
    column = block_column(shape, 1)
    source = lax.broadcasted_iota(jnp.int32, shape, 0)
    inner = column < HALF + HALO
    outer = column >= WIDE - HALO
    for out_ref, begin, wanted in (
        (first_ref, 0, jnp.where(inner, column, -1)),
        (second_ref, COLS - WIDE, jnp.where(column < HALF, column + LANES, jnp.where(outer, column - HALF, -1))),
    ):
        pick = one_hot(source == wanted)
        cut = slice(begin, begin + WIDE)
        out_ref[0 : SLABS - 1] = pick_columns([part[:, cut] for part in parts], pick).reshape(SLABS - 1, 8, WIDE)
        out_ref[SLABS - 1] = pick_columns([ids[:, cut]], pick)
        out_ref[SLABS - 1, :, FLAG_LANE : FLAG_LANE + SNAPS] = sup_ref[...].astype(jnp.float32)


def halo_kernel(side_ref, first_ref, second_ref, left_ref, right_ref, *out_refs):
    turn = row_major()
    shape = (LANES, WIDE)
    column = block_column(shape, 1)
    source = lax.broadcasted_iota(jnp.int32, shape, 0)
    blocks = []
    for in_ref, edge_ref, hit in (
        (first_ref, left_ref, (column >= WIDE - HALO) & (source == column - HALF)),
        (second_ref, right_ref, (column >= HALF) & (column < HALF + HALO) & (source == column - HALF)),
    ):
        pick = one_hot(hit)
        parts = turn_rows(halves(edge_ref[0:RESP].reshape(RESP * ROWS, LANES)), turn)
        fields = in_ref[0 : SLABS - 1] + pick_columns(parts, pick).reshape(SLABS - 1, 8, WIDE)
        ids = in_ref[SLABS - 1] + pick_columns([edge_ref[RESP].astype(jnp.bfloat16)], pick)
        blocks.append((fields, ids))
    low_side = side_ref[0] == 0
    (fields_0, ids_0), (fields_1, ids_1) = blocks
    near = NEAR * SETS
    keep_s_ref, keep_a_ref, far_keep_ref, give_s_ref, give_a_ref, far_give_ref = out_refs
    for sens_ref, act_ref, far_ref, fields, ids in (
        (keep_s_ref, keep_a_ref, far_keep_ref, jnp.where(low_side, fields_0, fields_1), jnp.where(low_side, ids_0, ids_1)),
        (
            give_s_ref, give_a_ref, far_give_ref,
            jnp.where(low_side, fields_1, fields_0), jnp.where(low_side, ids_1, ids_0),
        ),
    ):
        grid = fields.reshape(ROWS, SETS, 8, WIDE)
        act_ref[...] = grid[:, :ACT_SETS].reshape(ACT_SLABS, 8, WIDE)
        sens_ref[0:ROWS] = grid[:, ACT_SETS]
        sens_ref[ROWS] = ids
        far_ref[0:near] = jnp.where(low_side, fields[:near], fields[SLABS - 1 - near :])
        far_ref[near] = ids


def after(cells):
    return jnp.concatenate([cells[:, LANES:], pltpu.roll(cells[:, :LANES], LANES - 1, 1)], axis=1)


def strip_bases(side):
    return [OWN + shift + spot for shift in (0, -16, 16) for spot in (8 * side, 8 - 8 * side)]


def fill(side, strips, far, sets, offset, p_ref, u_ref, mk_ref):
    def place(slab, row, spot):
        begin = slab * (mk_ref[row] * (DT / (0.5 * DT * DT)))
        u_ref[spot] = begin
        p_ref[spot] = begin

    for ref, base in zip(strips, strip_bases(side)):
        for row in range(ROWS):
            for index in range(sets):
                place(ref[row * sets + index], base + row, (base + row) * sets + index)
    for ref, above in zip(far, (side, 1 - side)):
        base = above * (8 - NEAR) + (ALL_ROWS - 8) * (1 - above)
        for row in range(NEAR):
            for index in range(sets):
                place(ref[row * SETS + offset + index], base + row, (base + row) * sets + index)


def step(count, sets, unroll, p_ref, u_ref, fx_ref, fy_ref, fw_ref, mk_ref):
    first = OWN - STEPS + 1 + count
    rows = CENTRE_ROWS + 2 * (STEPS - 1) - 2 * count

    def start(index):
        centre = p_ref[first * sets + index]
        north = fx_ref[first] * (centre - p_ref[(first - 1) * sets + index])
        return centre, north

    def one(row, carry):
        face = fx_ref[row + 1]
        along = fy_ref[row]
        back = fw_ref[row]
        mass = mk_ref[row]
        done = []
        for index, (centre, north) in enumerate(carry):
            spot = row * sets + index
            below = p_ref[spot + sets]
            south = face * (below - centre)
            east = along * (after(centre) - centre)
            first_west = back * (centre[:, :LANES] - pltpu.roll(centre[:, WIDE - LANES :], 1, 1))
            west = jnp.concatenate([first_west, east[:, : WIDE - LANES]], axis=1)
            speed = u_ref[spot] + mass * ((south - north) + (east - west))
            u_ref[spot] = speed
            p_ref[spot] = centre + speed
            done.append((below, south))
        return tuple(done)

    def several(turn, carry):
        row = first + unroll * turn
        for extra in range(unroll):
            carry = one(row + extra, carry)
        return carry

    lax.fori_loop(0, (rows + unroll - 1) // unroll, several, tuple(start(index) for index in range(sets)))


def march(sets, unroll, keep_row, mask_ref, p_ref, u_ref, *faces):
    def snapshot(index):
        for strip in range(2):
            mask = jnp.broadcast_to(mask_ref[strip, pl.ds(index, 1), :], (8, WIDE))
            fast = mask * (1.0 / DT)

            def keep_rows(turn, carry, strip=strip, mask=mask, fast=fast):
                for extra in range(4):
                    at = turn * 4 + extra + 8 * strip
                    keep_row(index, at, (OWN + at) * sets, mask, fast)
                return carry

            lax.fori_loop(0, 2, keep_rows, 0)

    def advance(index, carry):
        step(2 * index, sets, unroll, p_ref, u_ref, *faces)
        step(2 * index + 1, sets, unroll, p_ref, u_ref, *faces)
        snapshot(index)
        return carry

    step(1, sets, unroll, p_ref, u_ref, *faces)
    snapshot(0)
    lax.fori_loop(1, SNAPS, advance, 0)


def in_order(side, sets, p_ref):
    shape = (WIDE, HALF)
    pick = one_hot(lax.broadcasted_iota(jnp.int32, shape, 1) == block_column(shape, 0))
    turn = row_major(8 * sets, inverse=True)
    for base in strip_bases(side)[:2]:
        cells = p_ref[pl.ds(base * sets, ROWS * sets)].reshape(ROWS * 8 * sets, WIDE)
        yield pick_columns(turn_rows(halves(cells), turn), pick).reshape(8 * sets, ROWS, HALF)


def sensor_kernel(
    side_ref, stiff_ref, dens_ref,
    keep_ref, give_ref, up_ref, dn_ref, far_keep_ref, far_give_ref,
    own_ref, other_ref, frames_ref, fx_ref, fy_ref, fw_ref, mk_ref, mask_ref,
    p_ref, u_ref, s_ref, m_ref,
):
    side = side_ref[0]
    strips = [keep_ref, give_ref]
    for ref in (up_ref, dn_ref):
        strips += [ref.at[0:SENS_SLABS], ref.at[SENS_SLABS:]]
    far = (far_keep_ref, far_give_ref)

    def materials(ids, base):
        stiff = jnp.zeros_like(ids)
        dens = jnp.zeros_like(ids)
        for region in range(REGIONS):
            here = ids == region + 1.0
            stiff = jnp.where(here, stiff_ref[region], stiff)
            dens = jnp.where(here, dens_ref[region], dens)
        inside = ids > 0.0
        rows = pl.ds(pl.multiple_of(base, 8), 8)
        s_ref[rows, :] = stiff
        m_ref[rows, :] = jnp.where(inside, (0.5 * DT * DT) / jnp.where(inside, dens, 1.0), 0.0)

    for ref, base in zip(strips, strip_bases(side)):
        materials(ref[ROWS], base)
    for ref, above in zip(far, (side, 1 - side)):
        materials(ref[FAR - 1], (ALL_ROWS - 8) * (1 - above))
    shape = (8, WIDE)
    tile = 4 * side + (block_column(shape, 1) >> 7)
    inside = block_column(shape, 1) < HALF
    spread = one_hot(inside & (lax.broadcasted_iota(jnp.int32, shape, 0) == tile))
    for ref, strip in ((keep_ref, side), (give_ref, 1 - side)):
        flags = ref[ROWS, :, 0:LANES].astype(jnp.bfloat16)
        masks = lax.dot_general(flags, spread, (((0,), (0,)), ((), ())), **FAST)
        mask_ref[strip] = masks[FLAG_LANE:LANES]

    def coefficients(turn, carry):
        for extra in range(9):
            row = 1 + turn * 9 + extra
            centre = jnp.broadcast_to(s_ref[pl.ds(row, 1), :], (8, WIDE))
            upper = jnp.broadcast_to(s_ref[pl.ds(row - 1, 1), :], (8, WIDE))
            fx_ref[row] = centre + upper
            fy_ref[row] = centre + after(centre)
            fw_ref[row] = centre[:, :LANES] + pltpu.roll(centre[:, WIDE - LANES :], 1, 1)
            mk_ref[row] = jnp.broadcast_to(m_ref[pl.ds(row, 1), :], (8, WIDE))
        return carry

    lax.fori_loop(0, (ALL_ROWS - 1) // 9, coefficients, 0)
    fill(side, strips, far, 1, ACT_SETS, p_ref, u_ref, mk_ref)

    def keep_row(index, at, spot, mask, fast):
        rows = pl.ds(pl.multiple_of(index * SENS, SENS), SENS)
        frames_ref[at, rows, 0:WIDE] = p_ref[spot] * mask
        frames_ref[at, rows, WIDE : 2 * WIDE] = u_ref[spot] * fast

    march(1, 16, keep_row, mask_ref, p_ref, u_ref, fx_ref, fy_ref, fw_ref, mk_ref)

    for out_ref, cells in zip((own_ref, other_ref), in_order(side, 1, p_ref)):
        out_ref[...] = cells


def actuator_kernel(
    side_ref, place_ref,
    keep_ref, give_ref, up_ref, dn_ref, far_keep_ref, far_give_ref,
    own_sens_ref, other_sens_ref, frames_ref, fx_ref, fy_ref, fw_ref, mk_ref, mask_ref,
    own_ref, other_ref, piece_0_ref, piece_1_ref, piece_2_ref, piece_3_ref,
    p_ref, u_ref, fa_ref, acc_ref,
):
    side = side_ref[0]
    strips = [keep_ref, give_ref]
    for ref in (up_ref, dn_ref):
        strips += [ref.at[0:ACT_SLABS], ref.at[ACT_SLABS:]]
    fill(side, strips, (far_keep_ref, far_give_ref), ACT_SETS, 0, p_ref, u_ref, mk_ref)

    def keep_row(index, at, spot, mask, fast):
        rows = pl.ds(pl.multiple_of(index * ACT, ACT), ACT)
        place = jnp.concatenate([p_ref[spot] * mask, p_ref[spot + 1] * mask], axis=0)
        speed = jnp.concatenate([u_ref[spot] * fast, u_ref[spot + 1] * fast], axis=0)
        fa_ref[at, rows, 0:WIDE] = place.astype(jnp.bfloat16)
        fa_ref[at, rows, WIDE : 2 * WIDE] = speed.astype(jnp.bfloat16)

    march(ACT_SETS, 6, keep_row, mask_ref, p_ref, u_ref, fx_ref, fy_ref, fw_ref, mk_ref)

    def gram(turn, total):
        for extra in range(4):
            row = 4 * turn + extra
            frames = frames_ref[row].astype(jnp.bfloat16)
            total = total + lax.dot_general(fa_ref[row], frames, (((1,), (1,)), ((), ())), **FAST)
        return total

    total = lax.fori_loop(0, CENTRE_ROWS // 4, gram, jnp.zeros((ACT * SNAPS, SENS * SNAPS), jnp.float32))
    shape = (ACT * SNAPS, ACT * SNAPS)
    old = lax.broadcasted_iota(jnp.int32, shape, 1)
    new = lax.broadcasted_iota(jnp.int32, shape, 0)
    turn = jnp.where(new == (old & (ACT - 1)) * SNAPS + (old >> 4), 1.0, 0.0)
    shape = (SENS * SNAPS, SENS * SNAPS)
    old = lax.broadcasted_iota(jnp.int32, shape, 0)
    new = lax.broadcasted_iota(jnp.int32, shape, 1)
    turn_back = jnp.where(new == (old & (SENS - 1)) * SNAPS + (old >> 3), 1.0, 0.0)
    turned = lax.dot_general(turn, total, MATMUL, **EXACT)
    acc_ref[...] = lax.dot_general(turned, turn_back, MATMUL, **EXACT) * (1.0 / math.sqrt(CELLS))
    place = place_ref[0]
    for hop, out_ref in enumerate((piece_0_ref, piece_1_ref, piece_2_ref, piece_3_ref)):
        out_ref[...] = acc_ref[pl.ds(pl.multiple_of(((place + hop) & 3) * SHARE, 8), SHARE), :]
    for out_ref, cells, sens_ref in zip(
        (own_ref, other_ref), in_order(side, ACT_SETS, p_ref), (own_sens_ref, other_sens_ref)
    ):
        out_ref[0:ACT] = cells
        out_ref[ACT:RESP] = sens_ref[...]


def array(*shape, dtype=jnp.float32):
    return jax.ShapeDtypeStruct(shape, dtype)


def scratch(*shape, dtype=jnp.float32):
    return pltpu.VMEM(shape, dtype)


def call(kernel, scalars, operands, out_shape, scratch_shapes, mebibytes):
    vmem = pl.BlockSpec(memory_space=pltpu.VMEM)
    smem = pl.BlockSpec(memory_space=pltpu.SMEM)
    return pl.pallas_call(
        kernel,
        out_shape=out_shape,
        in_specs=[smem] * len(scalars) + [vmem] * len(operands),
        out_specs=(vmem,) * len(out_shape),
        scratch_shapes=scratch_shapes,
        compiler_params=grant(mebibytes),
    )(*scalars, *operands)


def join_kernel(first_ref, second_ref, out_ref):
    count = first_ref.shape[0]
    out_ref[0:count] = first_ref[...]
    out_ref[count:] = second_ref[...]


def joined(first, second):
    count = first.shape[0]
    return call(join_kernel, (), (first, second), (array(2 * count, 8, WIDE),), [], 8)[0]


def sensor_block(scalars, operands):
    face = array(ROOM, 8, WIDE)
    part = array(SENS, ROWS, HALF)
    return call(
        sensor_kernel, scalars, operands,
        (
            part, part, array(CENTRE_ROWS, SENS * SNAPS, 2 * WIDE),
            face, face, array(ROOM, 8, LANES), face, array(2, LANES - FLAG_LANE, WIDE),
        ),
        [
            scratch(ROOM, 8, WIDE), scratch(ROOM, 8, WIDE), scratch(ALL_ROWS, WIDE), scratch(ALL_ROWS, WIDE),
        ],
        28,
    )


def actuator_block(scalars, operands):
    part = array(RESP, ROWS, HALF)
    state = scratch(ROOM * ACT_SETS, 8, WIDE)
    return call(
        actuator_kernel, scalars, operands,
        (part, part) + (array(SHARE, SENS * SNAPS),) * 4,
        [
            state, state,
            scratch(CENTRE_ROWS, ACT * SNAPS, 2 * WIDE, dtype=jnp.bfloat16),
            scratch(ACT * SNAPS, SENS * SNAPS),
        ],
        36,
    )


def along_dom(cells, distance):
    count = lax.axis_size("dom")
    return lax.ppermute(cells, "dom", [(i, i + distance) for i in range(count) if 0 <= i + distance < count])


def outward(cells, distance):
    count = lax.axis_size("dom")
    pairs = [(i, i + distance if i % 2 else i - distance) for i in range(count)]
    return lax.ppermute(cells, "dom", [(i, j) for i, j in pairs if 0 <= j < count])


def grant(mebibytes):
    return pltpu.CompilerParams(vmem_limit_bytes=mebibytes << 20)


def swap(cells, bit):
    count = lax.axis_size("dom")
    return lax.ppermute(cells, "dom", [(i, i ^ bit) for i in range(count)])


def body(actuator_fields, sensor_fields, region_ids, stiffness_table, density_table, supported):
    side = lax.axis_index("dom") % 2
    side_word = side.astype(jnp.int32).reshape(1)
    place_word = lax.axis_index("sec").astype(jnp.int32).reshape(1)
    sections = lax.axis_size("sec")
    right_edge, left_edge = edges(actuator_fields, sensor_fields, region_ids)
    left = lax.ppermute(right_edge, "sec", [(i, i + 1) for i in range(sections - 1)])
    right = lax.ppermute(left_edge, "sec", [(i + 1, i) for i in range(sections - 1)])
    flags = jnp.transpose(supported, (1, 2, 0)).reshape(-1, SNAPS)

    vmem = pl.BlockSpec(memory_space=pltpu.VMEM)
    smem = pl.BlockSpec(memory_space=pltpu.SMEM)
    block = jax.ShapeDtypeStruct((SLABS, 8, WIDE), jnp.float32)
    first, second = pl.pallas_call(
        main_kernel, out_shape=(block, block), in_specs=[vmem] * 4, out_specs=(vmem, vmem), compiler_params=grant(16)
    )(actuator_fields, sensor_fields, region_ids, flags)
    far = array(FAR, 8, WIDE)
    outs = (array(SENS_SLABS, 8, WIDE), array(ACT_SLABS, 8, WIDE), far)
    keep_s, keep_a, far_keep, give_s, give_a, far_give = call(
        halo_kernel, (side_word,), (first, second, left, right), outs + outs, [], 16
    )

    got_s = swap(give_s, 1)
    got_a = swap(give_a, 1)
    far_keep = outward(far_keep, 4)
    far_give = outward(far_give, 3)
    both_s = joined(keep_s, got_s)
    up_s = along_dom(both_s, 2)
    dn_s = along_dom(both_s, -2)
    both_a = joined(keep_a, got_a)
    up_a = along_dom(both_a, 2)
    dn_a = along_dom(both_a, -2)
    far = (far_keep, far_give)
    sensor = sensor_block((side_word, stiffness_table, density_table), (keep_s, got_s, up_s, dn_s) + far)
    own, other, *pieces = actuator_block((side_word, place_word), (keep_a, got_a, up_a, dn_a) + far + tuple(sensor))
    total = pieces[0]
    for hop in range(1, sections):
        total = total + lax.ppermute(pieces[hop], "sec", [(i, (i + hop) % sections) for i in range(sections)])
    other, total = lax.optimization_barrier((other, total))
    back = swap(other, 1)
    for bits in (4, 12, 16, 48):
        total = total + swap(total, bits)
    position = jnp.where(side == 0, jnp.concatenate([own, back], 2), jnp.concatenate([back, own], 2))
    total = total + sum(swap(total, bits) for bits in (1, 2, 3))
    return (position, total)


def solution(mesh):
    in_specs = (
        P(None, "dom", "sec"),
        P(None, "dom", "sec"),
        P("dom", "sec"),
        P(),
        P(),
        P(None, "dom", "sec"),
    )
    out_specs = (P(None, "dom", "sec"), P("sec", None))
    return jax.shard_map(body, mesh=mesh, in_specs=in_specs, out_specs=out_specs, check_vma=False)
```

```python
import math

import jax
import jax.numpy as jnp
from jax import lax
from jax.experimental import pallas as pl
from jax.experimental.pallas import tpu as pltpu
from jax.sharding import PartitionSpec as P


ROWS = 8
COLS = 1024
HALF = 512
LANES = 128
TILES = 5
WIDE = TILES * LANES
HALO = 20
ACT = 16
SENS = 8
RESP = ACT + SENS
SETS = RESP // 8
SNAPS = 10
STEPS = 20
REGIONS = 16
SLABS = ROWS * SETS + 1
NEAR = 3
FAR = NEAR * SETS + 1
OWN = 24
SHARE = 40
CELLS = 512 * 4096
FLAG_LANE = 112
ACT_SETS = ACT // 8
CENTRE_ROWS = 2 * ROWS
SENS_SLABS = ROWS + 1
ACT_SLABS = ROWS * ACT_SETS
ALL_ROWS = 64
ROOM = 80
DT = 0.35


def block_column(shape, dim):
    spot = lax.broadcasted_iota(jnp.int32, shape, dim)
    return (spot & (LANES - 1)) * TILES + (spot >> 7)


MATMUL = (((1,), (0,)), ((), ()))
FAST = dict(preferred_element_type=jnp.float32)
EXACT = dict(precision=lax.Precision.HIGHEST, preferred_element_type=jnp.float32)


def one_hot(hit):
    return jnp.where(hit, 1.0, 0.0).astype(jnp.bfloat16)


def halves(cells):
    high = cells.astype(jnp.bfloat16)
    return high, (cells - high.astype(jnp.float32)).astype(jnp.bfloat16)


def pick_columns(parts, pick):
    return sum(lax.dot_general(part, pick, MATMUL, **FAST) for part in parts)


def turn_rows(parts, turn):
    return [lax.dot_general(turn, part, MATMUL, **FAST).astype(jnp.bfloat16) for part in parts]


def row_major(count=RESP, inverse=False):
    shape = (ROWS * count, ROWS * count)
    old = lax.broadcasted_iota(jnp.int32, shape, 0 if inverse else 1)
    new = lax.broadcasted_iota(jnp.int32, shape, 1 if inverse else 0)
    return one_hot(new == (old & (ROWS - 1)) * count + (old >> 3))


def edge_kernel(*refs):
    for act_ref, sens_ref, ids_ref, out_ref in (refs[0:3] + refs[6:7], refs[3:6] + refs[7:8]):
        out_ref[0:ACT] = act_ref[...]
        out_ref[ACT:RESP] = sens_ref[...]
        out_ref[RESP] = ids_ref[...].astype(jnp.float32) + 1.0


def edges(actuator_fields, sensor_fields, region_ids):
    def blocks(column):
        return [
            pl.BlockSpec((ACT, ROWS, LANES), lambda i, c=column: (0, 0, c)),
            pl.BlockSpec((SENS, ROWS, LANES), lambda i, c=column: (0, 0, c)),
            pl.BlockSpec((ROWS, LANES), lambda i, c=column: (0, c)),
        ]

    out = jax.ShapeDtypeStruct((RESP + 1, ROWS, LANES), jnp.float32)
    whole = pl.BlockSpec((RESP + 1, ROWS, LANES), lambda i: (0, 0, 0))
    fields = (actuator_fields, sensor_fields, region_ids)
    return pl.pallas_call(
        edge_kernel,
        grid=(1,),
        out_shape=(out, out),
        in_specs=blocks(COLS // LANES - 1) + blocks(0),
        out_specs=(whole, whole),
    )(*fields, *fields)


def main_kernel(act_ref, sens_ref, ids_ref, sup_ref, first_ref, second_ref):
    turn = row_major()
    cells = jnp.concatenate(
        [act_ref[...].reshape(ACT * ROWS, COLS), sens_ref[...].reshape(SENS * ROWS, COLS)], axis=0
    )
    parts = turn_rows(halves(cells), turn)
    ids = (ids_ref[...].astype(jnp.float32) + 1.0).astype(jnp.bfloat16)
    shape = (WIDE, WIDE)
    column = block_column(shape, 1)
    source = lax.broadcasted_iota(jnp.int32, shape, 0)
    inner = column < HALF + HALO
    outer = column >= WIDE - HALO
    for out_ref, begin, wanted in (
        (first_ref, 0, jnp.where(inner, column, -1)),
        (second_ref, COLS - WIDE, jnp.where(column < HALF, column + LANES, jnp.where(outer, column - HALF, -1))),
    ):
        pick = one_hot(source == wanted)
        cut = slice(begin, begin + WIDE)
        out_ref[0 : SLABS - 1] = pick_columns([part[:, cut] for part in parts], pick).reshape(SLABS - 1, 8, WIDE)
        out_ref[SLABS - 1] = pick_columns([ids[:, cut]], pick)
        out_ref[SLABS - 1, :, FLAG_LANE : FLAG_LANE + SNAPS] = sup_ref[...].astype(jnp.float32)


def halo_kernel(side_ref, first_ref, second_ref, left_ref, right_ref, *out_refs):
    turn = row_major()
    shape = (LANES, WIDE)
    column = block_column(shape, 1)
    source = lax.broadcasted_iota(jnp.int32, shape, 0)
    blocks = []
    for in_ref, edge_ref, hit in (
        (first_ref, left_ref, (column >= WIDE - HALO) & (source == column - HALF)),
        (second_ref, right_ref, (column >= HALF) & (column < HALF + HALO) & (source == column - HALF)),
    ):
        pick = one_hot(hit)
        parts = turn_rows(halves(edge_ref[0:RESP].reshape(RESP * ROWS, LANES)), turn)
        fields = in_ref[0 : SLABS - 1] + pick_columns(parts, pick).reshape(SLABS - 1, 8, WIDE)
        ids = in_ref[SLABS - 1] + pick_columns([edge_ref[RESP].astype(jnp.bfloat16)], pick)
        blocks.append((fields, ids))
    low_side = side_ref[0] == 0
    (fields_0, ids_0), (fields_1, ids_1) = blocks
    near = NEAR * SETS
    keep_s_ref, keep_a_ref, far_keep_ref, give_s_ref, give_a_ref, far_give_ref = out_refs
    for sens_ref, act_ref, far_ref, fields, ids in (
        (keep_s_ref, keep_a_ref, far_keep_ref, jnp.where(low_side, fields_0, fields_1), jnp.where(low_side, ids_0, ids_1)),
        (
            give_s_ref, give_a_ref, far_give_ref,
            jnp.where(low_side, fields_1, fields_0), jnp.where(low_side, ids_1, ids_0),
        ),
    ):
        grid = fields.reshape(ROWS, SETS, 8, WIDE)
        act_ref[...] = grid[:, :ACT_SETS].reshape(ACT_SLABS, 8, WIDE)
        sens_ref[0:ROWS] = grid[:, ACT_SETS]
        sens_ref[ROWS] = ids
        far_ref[0:near] = jnp.where(low_side, fields[:near], fields[SLABS - 1 - near :])
        far_ref[near] = ids


def after(cells):
    return jnp.concatenate([cells[:, LANES:], pltpu.roll(cells[:, :LANES], LANES - 1, 1)], axis=1)


def strip_bases(side):
    return [OWN + shift + spot for shift in (0, -16, 16) for spot in (8 * side, 8 - 8 * side)]


def fill(side, strips, far, sets, offset, p_ref, u_ref, mk_ref):
    def place(slab, row, spot):
        begin = slab * (mk_ref[row] * (DT / (0.5 * DT * DT)))
        u_ref[spot] = begin
        p_ref[spot] = begin

    for ref, base in zip(strips, strip_bases(side)):
        for row in range(ROWS):
            for index in range(sets):
                place(ref[row * sets + index], base + row, (base + row) * sets + index)
    for ref, above in zip(far, (side, 1 - side)):
        base = above * (8 - NEAR) + (ALL_ROWS - 8) * (1 - above)
        for row in range(NEAR):
            for index in range(sets):
                place(ref[row * SETS + offset + index], base + row, (base + row) * sets + index)


def step(count, sets, unroll, p_ref, u_ref, fx_ref, fy_ref, fw_ref, mk_ref):
    first = OWN - STEPS + 1 + count
    rows = CENTRE_ROWS + 2 * (STEPS - 1) - 2 * count

    def start(index):
        centre = p_ref[first * sets + index]
        north = fx_ref[first] * (centre - p_ref[(first - 1) * sets + index])
        return centre, north

    def one(row, carry):
        face = fx_ref[row + 1]
        along = fy_ref[row]
        back = fw_ref[row]
        mass = mk_ref[row]
        done = []
        for index, (centre, north) in enumerate(carry):
            spot = row * sets + index
            below = p_ref[spot + sets]
            south = face * (below - centre)
            east = along * (after(centre) - centre)
            first_west = back * (centre[:, :LANES] - pltpu.roll(centre[:, WIDE - LANES :], 1, 1))
            west = jnp.concatenate([first_west, east[:, : WIDE - LANES]], axis=1)
            speed = u_ref[spot] + mass * ((south - north) + (east - west))
            u_ref[spot] = speed
            p_ref[spot] = centre + speed
            done.append((below, south))
        return tuple(done)

    def several(turn, carry):
        row = first + unroll * turn
        for extra in range(unroll):
            carry = one(row + extra, carry)
        return carry

    lax.fori_loop(0, (rows + unroll - 1) // unroll, several, tuple(start(index) for index in range(sets)))


def march(sets, unroll, keep_row, mask_ref, p_ref, u_ref, *faces):
    def snapshot(index):
        for strip in range(2):
            mask = jnp.broadcast_to(mask_ref[strip, pl.ds(index, 1), :], (8, WIDE))
            fast = mask * (1.0 / DT)

            def keep_rows(turn, carry, strip=strip, mask=mask, fast=fast):
                for extra in range(4):
                    at = turn * 4 + extra + 8 * strip
                    keep_row(index, at, (OWN + at) * sets, mask, fast)
                return carry

            lax.fori_loop(0, 2, keep_rows, 0)

    def advance(index, carry):
        step(2 * index, sets, unroll, p_ref, u_ref, *faces)
        step(2 * index + 1, sets, unroll, p_ref, u_ref, *faces)
        snapshot(index)
        return carry

    step(1, sets, unroll, p_ref, u_ref, *faces)
    snapshot(0)
    lax.fori_loop(1, SNAPS, advance, 0)


def in_order(side, sets, p_ref):
    shape = (WIDE, HALF)
    pick = one_hot(lax.broadcasted_iota(jnp.int32, shape, 1) == block_column(shape, 0))
    turn = row_major(8 * sets, inverse=True)
    for base in strip_bases(side)[:2]:
        cells = p_ref[pl.ds(base * sets, ROWS * sets)].reshape(ROWS * 8 * sets, WIDE)
        yield pick_columns(turn_rows(halves(cells), turn), pick).reshape(8 * sets, ROWS, HALF)


def sensor_kernel(
    side_ref, stiff_ref, dens_ref,
    keep_ref, give_ref, up_ref, dn_ref, far_keep_ref, far_give_ref,
    own_ref, other_ref, frames_ref, fx_ref, fy_ref, fw_ref, mk_ref, mask_ref,
    p_ref, u_ref, s_ref, m_ref,
):
    side = side_ref[0]
    strips = [keep_ref, give_ref]
    for ref in (up_ref, dn_ref):
        strips += [ref.at[0:SENS_SLABS], ref.at[SENS_SLABS:]]
    far = (far_keep_ref, far_give_ref)

    def materials(ids, base):
        stiff = jnp.zeros_like(ids)
        dens = jnp.zeros_like(ids)
        for region in range(REGIONS):
            here = ids == region + 1.0
            stiff = jnp.where(here, stiff_ref[region], stiff)
            dens = jnp.where(here, dens_ref[region], dens)
        inside = ids > 0.0
        rows = pl.ds(pl.multiple_of(base, 8), 8)
        s_ref[rows, :] = stiff
        m_ref[rows, :] = jnp.where(inside, (0.5 * DT * DT) / jnp.where(inside, dens, 1.0), 0.0)

    for ref, base in zip(strips, strip_bases(side)):
        materials(ref[ROWS], base)
    for ref, above in zip(far, (side, 1 - side)):
        materials(ref[FAR - 1], (ALL_ROWS - 8) * (1 - above))
    shape = (8, WIDE)
    tile = 4 * side + (block_column(shape, 1) >> 7)
    inside = block_column(shape, 1) < HALF
    spread = one_hot(inside & (lax.broadcasted_iota(jnp.int32, shape, 0) == tile))
    for ref, strip in ((keep_ref, side), (give_ref, 1 - side)):
        flags = ref[ROWS, :, 0:LANES].astype(jnp.bfloat16)
        masks = lax.dot_general(flags, spread, (((0,), (0,)), ((), ())), **FAST)
        mask_ref[strip] = masks[FLAG_LANE:LANES]

    def coefficients(turn, carry):
        for extra in range(9):
            row = 1 + turn * 9 + extra
            centre = jnp.broadcast_to(s_ref[pl.ds(row, 1), :], (8, WIDE))
            upper = jnp.broadcast_to(s_ref[pl.ds(row - 1, 1), :], (8, WIDE))
            fx_ref[row] = centre + upper
            fy_ref[row] = centre + after(centre)
            fw_ref[row] = centre[:, :LANES] + pltpu.roll(centre[:, WIDE - LANES :], 1, 1)
            mk_ref[row] = jnp.broadcast_to(m_ref[pl.ds(row, 1), :], (8, WIDE))
        return carry

    lax.fori_loop(0, (ALL_ROWS - 1) // 9, coefficients, 0)
    fill(side, strips, far, 1, ACT_SETS, p_ref, u_ref, mk_ref)

    def keep_row(index, at, spot, mask, fast):
        rows = pl.ds(pl.multiple_of(index * SENS, SENS), SENS)
        frames_ref[at, rows, 0:WIDE] = p_ref[spot] * mask
        frames_ref[at, rows, WIDE : 2 * WIDE] = u_ref[spot] * fast

    march(1, 16, keep_row, mask_ref, p_ref, u_ref, fx_ref, fy_ref, fw_ref, mk_ref)

    for out_ref, cells in zip((own_ref, other_ref), in_order(side, 1, p_ref)):
        out_ref[...] = cells


def actuator_kernel(
    side_ref, place_ref,
    keep_ref, give_ref, up_ref, dn_ref, far_keep_ref, far_give_ref,
    own_sens_ref, other_sens_ref, frames_ref, fx_ref, fy_ref, fw_ref, mk_ref, mask_ref,
    own_ref, other_ref, piece_0_ref, piece_1_ref, piece_2_ref, piece_3_ref,
    p_ref, u_ref, fa_ref, acc_ref,
):
    side = side_ref[0]
    strips = [keep_ref, give_ref]
    for ref in (up_ref, dn_ref):
        strips += [ref.at[0:ACT_SLABS], ref.at[ACT_SLABS:]]
    fill(side, strips, (far_keep_ref, far_give_ref), ACT_SETS, 0, p_ref, u_ref, mk_ref)

    def keep_row(index, at, spot, mask, fast):
        rows = pl.ds(pl.multiple_of(index * ACT, ACT), ACT)
        place = jnp.concatenate([p_ref[spot] * mask, p_ref[spot + 1] * mask], axis=0)
        speed = jnp.concatenate([u_ref[spot] * fast, u_ref[spot + 1] * fast], axis=0)
        fa_ref[at, rows, 0:WIDE] = place.astype(jnp.bfloat16)
        fa_ref[at, rows, WIDE : 2 * WIDE] = speed.astype(jnp.bfloat16)

    march(ACT_SETS, 6, keep_row, mask_ref, p_ref, u_ref, fx_ref, fy_ref, fw_ref, mk_ref)

    def gram(turn, total):
        for extra in range(8):
            row = 8 * turn + extra
            frames = frames_ref[row].astype(jnp.bfloat16)
            total = total + lax.dot_general(fa_ref[row], frames, (((1,), (1,)), ((), ())), **FAST)
        return total

    total = lax.fori_loop(0, CENTRE_ROWS // 8, gram, jnp.zeros((ACT * SNAPS, SENS * SNAPS), jnp.float32))
    shape = (ACT * SNAPS, ACT * SNAPS)
    old = lax.broadcasted_iota(jnp.int32, shape, 1)
    new = lax.broadcasted_iota(jnp.int32, shape, 0)
    turn = jnp.where(new == (old & (ACT - 1)) * SNAPS + (old >> 4), 1.0, 0.0)
    shape = (SENS * SNAPS, SENS * SNAPS)
    old = lax.broadcasted_iota(jnp.int32, shape, 0)
    new = lax.broadcasted_iota(jnp.int32, shape, 1)
    turn_back = jnp.where(new == (old & (SENS - 1)) * SNAPS + (old >> 3), 1.0, 0.0)
    turned = lax.dot_general(turn, total, MATMUL, **EXACT)
    acc_ref[...] = lax.dot_general(turned, turn_back, MATMUL, **EXACT) * (1.0 / math.sqrt(CELLS))
    place = place_ref[0]
    for hop, out_ref in enumerate((piece_0_ref, piece_1_ref, piece_2_ref, piece_3_ref)):
        out_ref[...] = acc_ref[pl.ds(pl.multiple_of(((place + hop) & 3) * SHARE, 8), SHARE), :]
    for out_ref, cells, sens_ref in zip(
        (own_ref, other_ref), in_order(side, ACT_SETS, p_ref), (own_sens_ref, other_sens_ref)
    ):
        out_ref[0:ACT] = cells
        out_ref[ACT:RESP] = sens_ref[...]


def array(*shape, dtype=jnp.float32):
    return jax.ShapeDtypeStruct(shape, dtype)


def scratch(*shape, dtype=jnp.float32):
    return pltpu.VMEM(shape, dtype)


def call(kernel, scalars, operands, out_shape, scratch_shapes, mebibytes):
    vmem = pl.BlockSpec(memory_space=pltpu.VMEM)
    smem = pl.BlockSpec(memory_space=pltpu.SMEM)
    return pl.pallas_call(
        kernel,
        out_shape=out_shape,
        in_specs=[smem] * len(scalars) + [vmem] * len(operands),
        out_specs=(vmem,) * len(out_shape),
        scratch_shapes=scratch_shapes,
        compiler_params=grant(mebibytes),
    )(*scalars, *operands)


def join_kernel(first_ref, second_ref, out_ref):
    count = first_ref.shape[0]
    out_ref[0:count] = first_ref[...]
    out_ref[count:] = second_ref[...]


def joined(first, second):
    count = first.shape[0]
    return call(join_kernel, (), (first, second), (array(2 * count, 8, WIDE),), [], 8)[0]


def sensor_block(scalars, operands):
    face = array(ROOM, 8, WIDE)
    part = array(SENS, ROWS, HALF)
    return call(
        sensor_kernel, scalars, operands,
        (
            part, part, array(CENTRE_ROWS, SENS * SNAPS, 2 * WIDE),
            face, face, array(ROOM, 8, LANES), face, array(2, LANES - FLAG_LANE, WIDE),
        ),
        [
            scratch(ROOM, 8, WIDE), scratch(ROOM, 8, WIDE), scratch(ALL_ROWS, WIDE), scratch(ALL_ROWS, WIDE),
        ],
        28,
    )


def actuator_block(scalars, operands):
    part = array(RESP, ROWS, HALF)
    state = scratch(ROOM * ACT_SETS, 8, WIDE)
    return call(
        actuator_kernel, scalars, operands,
        (part, part) + (array(SHARE, SENS * SNAPS),) * 4,
        [
            state, state,
            scratch(CENTRE_ROWS, ACT * SNAPS, 2 * WIDE, dtype=jnp.bfloat16),
            scratch(ACT * SNAPS, SENS * SNAPS),
        ],
        36,
    )


def along_dom(cells, distance):
    count = lax.axis_size("dom")
    return lax.ppermute(cells, "dom", [(i, i + distance) for i in range(count) if 0 <= i + distance < count])


def outward(cells, distance):
    count = lax.axis_size("dom")
    pairs = [(i, i + distance if i % 2 else i - distance) for i in range(count)]
    return lax.ppermute(cells, "dom", [(i, j) for i, j in pairs if 0 <= j < count])


def grant(mebibytes):
    return pltpu.CompilerParams(vmem_limit_bytes=mebibytes << 20)


def swap(cells, bit):
    count = lax.axis_size("dom")
    return lax.ppermute(cells, "dom", [(i, i ^ bit) for i in range(count)])


def body(actuator_fields, sensor_fields, region_ids, stiffness_table, density_table, supported):
    side = lax.axis_index("dom") % 2
    side_word = side.astype(jnp.int32).reshape(1)
    place_word = lax.axis_index("sec").astype(jnp.int32).reshape(1)
    sections = lax.axis_size("sec")
    right_edge, left_edge = edges(actuator_fields, sensor_fields, region_ids)
    left = lax.ppermute(right_edge, "sec", [(i, i + 1) for i in range(sections - 1)])
    right = lax.ppermute(left_edge, "sec", [(i + 1, i) for i in range(sections - 1)])
    flags = jnp.transpose(supported, (1, 2, 0)).reshape(-1, SNAPS)

    vmem = pl.BlockSpec(memory_space=pltpu.VMEM)
    smem = pl.BlockSpec(memory_space=pltpu.SMEM)
    block = jax.ShapeDtypeStruct((SLABS, 8, WIDE), jnp.float32)
    first, second = pl.pallas_call(
        main_kernel, out_shape=(block, block), in_specs=[vmem] * 4, out_specs=(vmem, vmem), compiler_params=grant(16)
    )(actuator_fields, sensor_fields, region_ids, flags)
    far = array(FAR, 8, WIDE)
    outs = (array(SENS_SLABS, 8, WIDE), array(ACT_SLABS, 8, WIDE), far)
    keep_s, keep_a, far_keep, give_s, give_a, far_give = call(
        halo_kernel, (side_word,), (first, second, left, right), outs + outs, [], 16
    )

    got_s = swap(give_s, 1)
    got_a = swap(give_a, 1)
    far_keep = outward(far_keep, 4)
    far_give = outward(far_give, 3)
    both_s = joined(keep_s, got_s)
    up_s = along_dom(both_s, 2)
    dn_s = along_dom(both_s, -2)
    both_a = joined(keep_a, got_a)
    up_a = along_dom(both_a, 2)
    dn_a = along_dom(both_a, -2)
    far = (far_keep, far_give)
    sensor = sensor_block((side_word, stiffness_table, density_table), (keep_s, got_s, up_s, dn_s) + far)
    own, other, *pieces = actuator_block((side_word, place_word), (keep_a, got_a, up_a, dn_a) + far + tuple(sensor))
    total = pieces[0]
    for hop in range(1, sections):
        total = total + lax.ppermute(pieces[hop], "sec", [(i, (i + hop) % sections) for i in range(sections)])
    other, total = lax.optimization_barrier((other, total))
    back = swap(other, 1)
    for bits in (4, 12, 16, 48):
        total = total + swap(total, bits)
    position = jnp.where(side == 0, jnp.concatenate([own, back], 2), jnp.concatenate([back, own], 2))
    total = total + sum(swap(total, bits) for bits in (1, 2, 3))
    return (position, total)


def solution(mesh):
    in_specs = (
        P(None, "dom", "sec"),
        P(None, "dom", "sec"),
        P("dom", "sec"),
        P(),
        P(),
        P(None, "dom", "sec"),
    )
    out_specs = (P(None, "dom", "sec"), P("sec", None))
    return jax.shard_map(body, mesh=mesh, in_specs=in_specs, out_specs=out_specs, check_vma=False)
```
